256 devices in a mesh: seq: 32 (over z, x_lo, core), dp: 8 (over y, x_hi).
Axes of the slice: x: 4 (x_hi: 2, x_lo: 2; x = x_hi * 2 + x_lo), y: 4, z: 8, core: 2. Of those that a mesh axis runs over, the one named last changes fastest.
Arguments:
- queries: bfloat16 [8, 4096, 2048], P('dp', 'seq'), may hold values from -18 to 18
- key_vectors: bfloat16 [8, 4096, 2048], P('dp', 'seq'), may hold values from -18 to 18
- value_vectors: bfloat16 [8, 4096, 2048], P('dp', 'seq'), may hold values from -6 to 6
- cotangent: bfloat16 [8, 4096, 2048], P('dp', 'seq'), may hold values from -6 to 6
- compress_kernel: bfloat16 [512, 128], replicated, may hold values from -0.25 to 0.25
- memory_reach: int32 [8, 32], P('dp', 'seq'), may hold values from 1 to 4, as said below
Outputs:
- attended: bfloat16 [8, 4096, 2048], P('dp', 'seq')
- grad_queries: bfloat16 [8, 4096, 2048], P('dp', 'seq')
- grad_keys: bfloat16 [8, 4096, 2048], P('dp', 'seq')
- grad_values: bfloat16 [8, 4096, 2048], P('dp', 'seq')
- grad_kernel: float32 [512, 128], P('seq')
The draws below stay inside these ranges and needn't reach their ends.
Inputs may be any that keep to these rules, and one draw needn't show every extreme that they name: `memory_reach`: some segment reads 4 earlier segments and some reads 1.
All inputs are finite; a program needn't handle non-finite values.
Results may differ from the reference program's by a relative error of at most 0.0076.
Values may be sent and summed in bfloat16 or wider, within the bound.
A program may use at most 64 MiB of HBM per device.

```python
import jax
import jax.numpy as jnp
from jax import lax

H = 16
E = 128
SEG = 128
SEGMENTS = 32
LEN = 4096
BOOKS = 8


def query_key_pair(key):
    shape_full = (BOOKS, LEN, H, E)
    query_full = jax.random.normal(jax.random.fold_in(key, 311), shape_full, jnp.float32)
    key_full = jax.random.normal(jax.random.fold_in(key, 312), shape_full, jnp.float32)
    query_full = jnp.clip(query_full, -18.0, 18.0).reshape(BOOKS, LEN, H * E)
    key_full = jnp.clip(key_full, -18.0, 18.0).reshape(BOOKS, LEN, H * E)
    return (query_full, key_full)


def draw_queries(key, part):
    return query_key_pair(key)[0].astype(jnp.bfloat16)


def draw_key_vectors(key, part):
    return query_key_pair(key)[1].astype(jnp.bfloat16)


def draw_memory_reach(key, part):
    counted = BOOKS * SEGMENTS
    drawn = jax.random.randint(jax.random.fold_in(key, 401), (counted,), 1, 5, dtype=jnp.int32)
    chosen_top = jax.random.randint(jax.random.fold_in(key, 402), (), 0, counted, dtype=jnp.int32)
    chosen_low = (chosen_top + 1) % counted
    flat_ids = jnp.arange(counted, dtype=jnp.int32)
    drawn = jnp.where(flat_ids == chosen_top, 4, drawn)
    drawn = jnp.where(flat_ids == chosen_low, 1, drawn)
    return drawn.reshape(BOOKS, SEGMENTS).astype(jnp.int32)


def levels(key, dims, pieces, low, top_value):
    gain = 1.0
    for dim, shards_of in pieces:
        heights = jax.random.uniform(jax.random.fold_in(jax.random.fold_in(key, 6), dim), (shards_of,), jnp.float32, low / len(pieces), top_value / len(pieces))
        gain = gain * jnp.repeat(jnp.exp(heights), dims[dim] // shards_of).reshape((-1,) + (1,) * (len(dims) - 1 - dim))
    return gain


def scatter_about(key, extent, deviation, bound, cuts=(), kind=jnp.bfloat16):
    entries = jax.random.normal(key, extent, jnp.float32) * deviation
    if len(cuts) > 0:
        entries = levels(key, extent, cuts, -0.22, 0.18) * entries
    return jnp.clip(entries, min=-bound, max=bound).astype(kind)


def setup_inputs(seed: int = 0) -> dict:
    seeds = jax.random.split(jax.random.key(seed), 7)
    queries = draw_queries(jax.random.fold_in(seeds[6], 71), 0)
    key_vectors = draw_key_vectors(jax.random.fold_in(seeds[6], 71), 0)
    value_vectors = scatter_about(seeds[2], (BOOKS, LEN, H * E), 1.0, 6.0, ((0, 8), (1, 32)))
    cotangent = scatter_about(seeds[3], (BOOKS, LEN, H * E), 1.0, 6.0, ((0, 8), (1, 32)))
    compress_kernel = scatter_about(seeds[4], (4 * E, E), (4 * E) ** -0.5, 0.25)
    memory_reach = draw_memory_reach(jax.random.fold_in(seeds[6], 71), 0)
    return dict(queries=queries, key_vectors=key_vectors, value_vectors=value_vectors, cotangent=cotangent, compress_kernel=compress_kernel, memory_reach=memory_reach)


def attend_block(query_rows, key_rows, value_rows, grad_rows, memory_keys, memory_values, visible):
    segment_len = query_rows.shape[0]
    slot_rows = segment_len // 4
    span_len = 2 * segment_len
    score_scale = E ** -0.5
    query_heads = query_rows.astype(jnp.float32).reshape(segment_len, H, E)
    grad_heads = grad_rows.astype(jnp.float32).reshape(segment_len, H, E)
    key_heads = jnp.concatenate([memory_keys, key_rows], 0).astype(jnp.float32).reshape(span_len, H, E)
    value_heads = jnp.concatenate([memory_values, value_rows], 0).astype(jnp.float32).reshape(span_len, H, E)
    columns = jnp.arange(span_len, dtype=jnp.int32)
    row_ids = jnp.arange(segment_len, dtype=jnp.int32)
    slot_of = jnp.minimum(columns // slot_rows, 3)
    memory_open = jnp.any((slot_of[:, None] == jnp.arange(4, dtype=jnp.int32)[None, :]) & visible[None, :], axis=1)
    allowed = jnp.where(columns[None, :] < segment_len, memory_open[None, :], columns[None, :] - segment_len <= row_ids[:, None])
    scores = jnp.einsum("shd,lhd->hsl", query_heads, key_heads) * score_scale
    scores = jnp.where(allowed[None], scores, -1e30)
    highest = jnp.max(scores, axis=2, keepdims=True)
    raised = jnp.where(allowed[None], jnp.exp(scores - highest), 0.0)
    weights = raised / jnp.sum(raised, axis=2, keepdims=True)
    weights_low = lax.optimization_barrier(weights.astype(jnp.bfloat16)).astype(jnp.float32)
    attended = jnp.einsum("hsl,lhd->shd", weights_low, value_heads)
    grad_weights = jnp.einsum("shd,lhd->hsl", grad_heads, value_heads)
    row_delta = jnp.sum(weights * grad_weights, axis=2, keepdims=True)
    grad_scores = (weights * (grad_weights - row_delta) * score_scale).astype(jnp.bfloat16)
    grad_scores = lax.optimization_barrier(grad_scores).astype(jnp.float32)
    grad_query = jnp.einsum("hsl,lhd->shd", grad_scores, key_heads)
    grad_key_list = jnp.einsum("hsl,shd->lhd", grad_scores, query_heads).reshape(span_len, H * E)
    grad_value_list = jnp.einsum("hsl,shd->lhd", weights_low, grad_heads).reshape(span_len, H * E)
    return (attended.reshape(segment_len, H * E).astype(jnp.bfloat16),
            grad_query.reshape(segment_len, H * E).astype(jnp.bfloat16),
            grad_key_list[segment_len:], grad_value_list[segment_len:],
            grad_key_list[:segment_len], grad_value_list[:segment_len])


def reference(queries, key_vectors, value_vectors, cotangent, compress_kernel, memory_reach):
    slot_rows = SEG // 4
    head_width = H * E
    kernel = compress_kernel.reshape(4, E, E).astype(jnp.float32)
    key_blocks = key_vectors.reshape(BOOKS, SEGMENTS, slot_rows, 4, H, E).astype(jnp.float32)
    value_blocks = value_vectors.reshape(BOOKS, SEGMENTS, slot_rows, 4, H, E).astype(jnp.float32)
    packed_keys = jnp.einsum("bsmthe,tef->bsmhf", key_blocks, kernel).astype(jnp.bfloat16)
    packed_values = jnp.einsum("bsmthe,tef->bsmhf", value_blocks, kernel).astype(jnp.bfloat16)
    packed_keys = packed_keys.reshape(BOOKS, SEGMENTS, slot_rows, head_width)
    packed_values = packed_values.reshape(BOOKS, SEGMENTS, slot_rows, head_width)
    padded_keys = jnp.pad(packed_keys, ((0, 0), (4, 0), (0, 0), (0, 0)))
    padded_values = jnp.pad(packed_values, ((0, 0), (4, 0), (0, 0), (0, 0)))
    zero_index = jnp.zeros((), jnp.int32)
    slot_ids = jnp.arange(1, 5, dtype=jnp.int32)

    def one_segment(index):
        book_id = (index // SEGMENTS).astype(jnp.int32)
        segment_id = (index % SEGMENTS).astype(jnp.int32)
        first_row = (segment_id * SEG).astype(jnp.int32)

        def rows_of(array):
            return lax.dynamic_slice(array, (book_id, first_row, zero_index), (1, SEG, head_width))[0]

        def memory_of(array):
            picked = lax.dynamic_slice(array, (book_id, segment_id, zero_index, zero_index), (1, 4, slot_rows, head_width))[0]
            return picked[::-1].reshape(4 * slot_rows, head_width)

        reach_here = lax.dynamic_slice(memory_reach, (book_id, segment_id), (1, 1))[0, 0]
        visible = (slot_ids <= reach_here) & (segment_id - slot_ids >= 0)
        return attend_block(rows_of(queries), rows_of(key_vectors), rows_of(value_vectors), rows_of(cotangent),
                            memory_of(padded_keys), memory_of(padded_values), visible)

    results = lax.map(one_segment, jnp.arange(BOOKS * SEGMENTS, dtype=jnp.int32))
    attended = results[0].reshape(BOOKS, LEN, head_width)
    grad_queries = results[1].reshape(BOOKS, LEN, head_width)
    local_keys = results[2].reshape(BOOKS, LEN, head_width)
    local_values = results[3].reshape(BOOKS, LEN, head_width)

    def gather_back(grads):
        shaped = grads.reshape(BOOKS, SEGMENTS, 4, slot_rows, head_width)
        padded = jnp.pad(shaped, ((0, 0), (0, 4), (0, 0), (0, 0), (0, 0)))
        summed = jnp.zeros((BOOKS, SEGMENTS, slot_rows, head_width), jnp.float32)
        for offset in range(1, 5):
            summed = summed + padded[:, offset:offset + SEGMENTS, offset - 1]
        rounded = lax.optimization_barrier(summed.astype(jnp.bfloat16))
        return rounded.astype(jnp.float32).reshape(BOOKS, SEGMENTS, slot_rows, H, E)

    memory_grad_keys = gather_back(results[4])
    memory_grad_values = gather_back(results[5])
    back_keys = jnp.einsum("bsmhf,tef->bsmthe", memory_grad_keys, kernel).reshape(BOOKS, LEN, head_width)
    back_values = jnp.einsum("bsmhf,tef->bsmthe", memory_grad_values, kernel).reshape(BOOKS, LEN, head_width)
    grad_keys = (local_keys + back_keys).astype(jnp.bfloat16)
    grad_values = (local_values + back_values).astype(jnp.bfloat16)
    grad_kernel = (jnp.einsum("bsmthe,bsmhf->tef", key_blocks, memory_grad_keys)
                   + jnp.einsum("bsmthe,bsmhf->tef", value_blocks, memory_grad_values)).reshape(4 * E, E)
    return (attended, grad_queries, grad_keys, grad_values, grad_kernel)
```

```python
import functools

import jax
import jax.numpy as jnp
from jax import lax
from jax.experimental import pallas as pl
from jax.experimental.pallas import tpu as pltpu
from jax.sharding import PartitionSpec as P

MESH = pl.DeviceIdType.MESH
H = 16
E = 128
SEG = 128
ROWS = SEG // 4
SLOTS = 4
HC = 4
NC = H // HC
WIDTH = H * E
BF = jnp.bfloat16
F32 = jnp.float32
SCALE = E ** -0.5
LOG2E = 1.4426950408889634
S1, S2, R1, R3, T1, T3, U1, U2 = range(8)


def nn(a, b):
    return lax.dot_general(a, b, (((1,), (0,)), ((), ())), preferred_element_type=F32)


def nt(a, b):
    return lax.dot_general(a, b, (((1,), (1,)), ((), ())), preferred_element_type=F32)


def tn(a, b):
    return lax.dot_general(a, b, (((0,), (0,)), ((), ())), preferred_element_type=F32)


def kernel(
    chips, books,
    q_hbm, k_hbm, v_hbm, g_hbm, w_hbm, reach,
    att_hbm, gq_hbm, gk_hbm, gv_hbm, gw_hbm,
    q_in, k_in, v_in, g_in, w_in,
    k_perm, v_perm, stacked, memory, bias, perms,
    slot_grads, sibling, totals, arrived, own,
    att_out, gq_out, gk_out, gv_out, gw_out,
    kg_half, kg_pair, kg_sent, kg_got, kg_books,
    load_sem, store_sem, send_sem, recv_sem, ring_send, ring_recv, book_send, book_recv,
):
    me = lax.axis_index("seq")
    book = lax.axis_index("dp")
    chip = me // 2
    core = me % 2
    twin = me + 1 - 2 * core

    def chip_at(step):
        return ((chip + step + chips) % chips) * 2 + core

    loads = [
        pltpu.make_async_copy(source, target, load_sem.at[i])
        for i, (source, target) in enumerate([
            (k_hbm.at[0], k_in), (v_hbm.at[0], v_in), (w_hbm, w_in), (q_hbm.at[0], q_in), (g_hbm.at[0], g_in),
        ])
    ]
    for load in loads:
        load.start()

    barrier = pltpu.get_barrier_semaphore()

    def greet(**where):
        pl.semaphore_signal(barrier, inc=1, device_id=where, device_id_type=MESH)

    greet(seq=twin)
    for step in range(1, chips):
        greet(seq=chip_at(step))
    for step in range(1, books):
        greet(dp=(book + step) % books)

    def push(kind, chunk, source, target, device):
        return pltpu.make_async_remote_copy(
            src_ref=source, dst_ref=target, send_sem=send_sem.at[kind, chunk], recv_sem=recv_sem.at[kind, chunk],
            device_id={"seq": device}, device_id_type=MESH,
        )

    def heads(chunk):
        return pl.ds(chunk * HC, HC)

    def cols(head, count=1):
        return pl.ds(head * E, count * E)

    links = {}
    for c in range(NC):
        links[S1, c] = push(S1, c, memory.at[0, heads(c)], memory.at[2, heads(c)], chip_at(1))
        links[S2, c] = push(S2, c, memory.at[0, heads(c)], memory.at[4, heads(c)], chip_at(2))
        links[R1, c] = push(R1, c, memory.at[2 * core, heads(c)], memory.at[1, heads(c)], twin)
        links[R3, c] = push(R3, c, memory.at[2 + 2 * core, heads(c)], memory.at[3, heads(c)], twin)
        links[T1, c] = push(T1, c, slot_grads.at[0, heads(c)], sibling.at[1 - core, heads(c)], twin)
        links[T3, c] = push(T3, c, slot_grads.at[2, heads(c)], sibling.at[2 - core, heads(c)], twin)
        links[U1, c] = push(U1, c, totals.at[0, heads(c)], arrived.at[0, heads(c)], chip_at(-1))
        links[U2, c] = push(U2, c, totals.at[1, heads(c)], arrived.at[1, heads(c)], chip_at(-2))

    sibling[2 - 2 * core] = jnp.zeros((H, 2 * ROWS, E), BF)

    row = lax.broadcasted_iota(jnp.int32, (SEG, SEG), 0)
    col = lax.broadcasted_iota(jnp.int32, (SEG, SEG), 1)
    row_key = 4 * (row % ROWS) + row // ROWS
    col_key = 4 * (col % ROWS) + col // ROWS
    perms[0] = jnp.where(col == row_key, 1.0, 0.0).astype(BF)
    perms[1] = jnp.where(row == col_key, 1.0, 0.0).astype(BF)
    slot = row // ROWS + 1
    seen = jnp.minimum(reach[0, 0], me)
    bias[0:SEG] = jnp.where(slot <= seen, 0.0, -1e30)
    bias[SEG:] = jnp.where(row_key <= col, 0.0, -1e30)

    def compress(c):
        span = cols(c * HC, HC)
        rows = []
        for source, target in ((k_in, k_perm), (v_in, v_perm)):
            moved = nn(perms[0], source[:, span]).astype(BF)
            for h in range(HC):
                one = moved[:, h * E:(h + 1) * E]
                target[c * HC + h] = one
                rows.append(jnp.concatenate([one[t * ROWS:(t + 1) * ROWS] for t in range(4)], axis=1))
        lhs = jnp.concatenate(rows, axis=0)
        stacked[c] = lhs
        packed = nn(lhs, w_in[...]).astype(BF)
        for h in range(HC):
            memory[0, c * HC + h, 0:ROWS] = packed[h * ROWS:(h + 1) * ROWS]
            memory[0, c * HC + h, ROWS:] = packed[(HC + h) * ROWS:(HC + h + 1) * ROWS]

    def attend(h):
        keys = jnp.concatenate([memory[r, h, 0:ROWS] for r in range(1, 5)] + [k_perm[h]], axis=0)
        values = jnp.concatenate([memory[r, h, ROWS:] for r in range(1, 5)] + [v_perm[h]], axis=0)
        query = q_in[:, cols(h)]
        grad = g_in[:, cols(h)]
        scores = nt(keys, query) * (SCALE * LOG2E) + bias[...]
        raised = jnp.exp2(scores - jnp.max(scores, axis=0, keepdims=True))
        weights = raised * (1.0 / jnp.sum(raised, axis=0, keepdims=True))
        low = weights.astype(BF)
        grad_weights = nt(values, grad)
        delta = jnp.sum(weights * grad_weights, axis=0, keepdims=True)
        grad_scores = (weights * (grad_weights - delta) * SCALE).astype(BF)
        att_out[:, cols(h)] = tn(low, values).astype(BF)
        gq_out[:, cols(h)] = tn(grad_scores, keys).astype(BF)
        for i, terms in enumerate((nn(grad_scores, query), nn(low, grad))):
            own[i, h] = terms[SEG:]
            for r in range(SLOTS):
                slot_grads[r, h, i * ROWS:(i + 1) * ROWS] = terms[r * ROWS:(r + 1) * ROWS].astype(BF)

    def combine(c):
        links[T1, c].wait_recv()
        links[T3, c].wait_recv()
        for i in range(2):
            totals[i, heads(c)] = (
                slot_grads[2 * i + 1, heads(c)].astype(F32) + sibling[i + 1, heads(c)].astype(F32)
            ).astype(BF)
        links[U1, c].start()
        links[U2, c].start()

    def finish(c, kernel_terms):
        links[U1, c].wait_recv()
        links[U2, c].wait_recv()
        memory_grads = (
            arrived[0, heads(c)].astype(F32) + arrived[1, heads(c)].astype(F32) + sibling[0, heads(c)].astype(F32)
        ).astype(BF)
        rows = jnp.concatenate(
            [memory_grads[h, i * ROWS:(i + 1) * ROWS] for i in range(2) for h in range(HC)], axis=0
        )
        terms = tn(stacked[c], rows)
        back = nt(rows, w_in[...])
        for i, out in enumerate((gk_out, gv_out)):
            pieces = []
            for h in range(HC):
                first = (i * HC + h) * ROWS
                spread = jnp.concatenate(
                    [back[first:first + ROWS, t * E:(t + 1) * E] for t in range(4)], axis=0
                )
                pieces.append((own[i, c * HC + h] + spread).astype(BF))
            out[:, cols(c * HC, HC)] = nn(perms[1], jnp.concatenate(pieces, axis=1)).astype(BF)
        return terms if kernel_terms is None else kernel_terms + terms

    for load in loads[:3]:
        load.wait()
    for c in range(NC):
        compress(c)
        if c == 0:
            pl.semaphore_wait(barrier, chips + books - 1)
        links[S1, c].start()
        links[S2, c].start()
    for load in loads[3:]:
        load.wait()

    kernel_terms = None
    for c in range(NC):
        links[S1, c].wait_recv()
        links[S2, c].wait_recv()
        links[R1, c].start()
        links[R3, c].start()
        links[R1, c].wait_recv()
        links[R3, c].wait_recv()
        for h in range(HC):
            attend(c * HC + h)
        links[T1, c].start()
        links[T3, c].start()
        if c >= 1:
            combine(c - 1)
        if c >= 2:
            kernel_terms = finish(c - 2, kernel_terms)
    stores = [
        pltpu.make_async_copy(source, target, store_sem.at[i])
        for i, (source, target) in enumerate([
            (att_out, att_hbm.at[0]), (gq_out, gq_hbm.at[0]), (gk_out, gk_hbm.at[0]), (gv_out, gv_hbm.at[0]),
            (gw_out, gw_hbm),
        ])
    ]
    stores[0].start()
    stores[1].start()
    combine(NC - 1)
    for c in range(max(NC - 2, 0), NC):
        kernel_terms = finish(c, kernel_terms)

    share = 4 * E // (2 * chips)
    for i in range(2 * chips):
        kg_half[i % 2, i // 2] = kernel_terms[i * share:(i + 1) * share]
    swap = pltpu.make_async_remote_copy(
        src_ref=kg_half.at[1 - core], dst_ref=kg_pair, send_sem=ring_send.at[0], recv_sem=ring_recv.at[0],
        device_id={"seq": twin}, device_id_type=MESH,
    )
    swap.start()
    stores[2].start()
    stores[3].start()
    swap.wait_recv()
    kg_sent[...] = (kg_half[core] + kg_pair[...]).astype(BF)
    around = []
    for step in range(1, chips):
        around.append(pltpu.make_async_remote_copy(
            src_ref=kg_sent.at[(chip + step) % chips], dst_ref=kg_got.at[step],
            send_sem=ring_send.at[step], recv_sem=ring_recv.at[step],
            device_id={"seq": chip_at(step)}, device_id_type=MESH,
        ))
    for copy in around:
        copy.start()
    total = kg_sent[chip].astype(F32)
    for step, copy in enumerate(around):
        copy.wait_recv()
        total = total + kg_got[step + 1].astype(F32)
    kg_books[book] = total
    across = []
    for step in range(1, books):
        across.append(pltpu.make_async_remote_copy(
            src_ref=kg_books.at[book], dst_ref=kg_books.at[book],
            send_sem=book_send.at[step], recv_sem=book_recv.at[step],
            device_id={"dp": (book + step) % books}, device_id_type=MESH,
        ))
    for copy in across:
        copy.start()
    for copy in across:
        copy.wait_recv()
    whole = kg_books[0]
    for i in range(1, books):
        whole = whole + kg_books[i]
    gw_out[...] = whole
    stores[4].start()
    for c in range(NC):
        for kind in range(8):
            links[kind, c].wait_send()
    swap.wait_send()
    for copy in around + across:
        copy.wait_send()
    for store in stores:
        store.wait()


def solution(mesh):
    chips = mesh.shape["seq"] // 2
    books = mesh.shape["dp"]

    def local(queries, key_vectors, value_vectors, cotangent, compress_kernel, memory_reach):
        share = 4 * E // (2 * chips)
        rows = jax.ShapeDtypeStruct((1, SEG, WIDTH), BF)
        anywhere = pl.BlockSpec(memory_space=pl.ANY)
        vm = pltpu.VMEM
        return pl.pallas_call(
            functools.partial(kernel, chips, books),
            out_shape=(rows, rows, rows, rows, jax.ShapeDtypeStruct((share, E), F32)),
            in_specs=[anywhere] * 5 + [pl.BlockSpec(memory_space=pltpu.SMEM)],
            out_specs=[anywhere] * 5,
            scratch_shapes=[
                *[vm((SEG, WIDTH), BF)] * 4, vm((4 * E, E), BF),
                vm((H, SEG, E), BF), vm((H, SEG, E), BF), vm((NC, 2 * HC * ROWS, 4 * E), BF),
                vm((5, H, 2 * ROWS, E), BF), vm((2 * SEG, SEG), F32), vm((2, SEG, SEG), BF),
                vm((SLOTS, H, 2 * ROWS, E), BF), vm((3, H, 2 * ROWS, E), BF), vm((2, H, 2 * ROWS, E), BF),
                vm((2, H, 2 * ROWS, E), BF), vm((2, H, SEG, E), F32),
                *[vm((SEG, WIDTH), BF)] * 4, vm((share, E), F32),
                vm((2, chips, share, E), F32), vm((chips, share, E), F32), vm((chips, share, E), BF),
                vm((chips, share, E), BF), vm((books, share, E), F32),
                pltpu.SemaphoreType.DMA((5,)), pltpu.SemaphoreType.DMA((5,)),
                pltpu.SemaphoreType.DMA((8, NC)), pltpu.SemaphoreType.DMA((8, NC)),
                pltpu.SemaphoreType.DMA((chips,)), pltpu.SemaphoreType.DMA((chips,)),
                pltpu.SemaphoreType.DMA((books,)), pltpu.SemaphoreType.DMA((books,)),
            ],
            compiler_params=pltpu.CompilerParams(collective_id=0, has_side_effects=True),
        )(queries, key_vectors, value_vectors, cotangent, compress_kernel, memory_reach)

    rows = P("dp", "seq", None)
    return jax.shard_map(
        local, mesh=mesh, in_specs=(rows, rows, rows, rows, P(), P("dp", "seq")),
        out_specs=(rows, rows, rows, rows, P("seq", None)), check_vma=False,
    )
```

```python
import functools

import jax
import jax.numpy as jnp
from jax import lax
from jax.experimental import pallas as pl
from jax.experimental.pallas import tpu as pltpu
from jax.sharding import PartitionSpec as P

MESH = pl.DeviceIdType.MESH
H = 16
E = 128
SEG = 128
ROWS = SEG // 4
SLOTS = 4
HC = 4
NC = H // HC
WIDTH = H * E
BF = jnp.bfloat16
F32 = jnp.float32
SCALE = E ** -0.5
LOG2E = 1.4426950408889634
S1, S2, R1, R3, T1, T3, U1, U2 = range(8)


def nn(a, b):
    return lax.dot_general(a, b, (((1,), (0,)), ((), ())), preferred_element_type=F32)


def nt(a, b):
    return lax.dot_general(a, b, (((1,), (1,)), ((), ())), preferred_element_type=F32)


def tn(a, b):
    return lax.dot_general(a, b, (((0,), (0,)), ((), ())), preferred_element_type=F32)


def kernel(
    chips, books,
    q_hbm, k_hbm, v_hbm, g_hbm, w_hbm, reach,
    att_out, gq_out, gk_out, gv_out, gw_out,
    q_in, k_in, v_in, g_in, w_in,
    k_perm, v_perm, stacked, memory, bias, perms,
    slot_grads, sibling, totals, arrived, own,
    kg_half, kg_pair, kg_sent, kg_got, kg_books,
    load_sem, send_sem, recv_sem, ring_send, ring_recv, book_send, book_recv,
):
    me = lax.axis_index("seq")
    book = lax.axis_index("dp")
    chip = me // 2
    core = me % 2
    twin = me + 1 - 2 * core

    def chip_at(step):
        return ((chip + step + chips) % chips) * 2 + core

    loads = [
        pltpu.make_async_copy(source, target, load_sem.at[i])
        for i, (source, target) in enumerate([
            (k_hbm.at[0], k_in), (v_hbm.at[0], v_in), (w_hbm, w_in), (q_hbm.at[0], q_in), (g_hbm.at[0], g_in),
        ])
    ]
    for load in loads:
        load.start()

    barrier = pltpu.get_barrier_semaphore()

    def greet(**where):
        pl.semaphore_signal(barrier, inc=1, device_id=where, device_id_type=MESH)

    greet(seq=twin)
    for step in range(1, chips):
        greet(seq=chip_at(step))
    for step in range(1, books):
        greet(dp=(book + step) % books)

    def push(kind, chunk, source, target, device):
        return pltpu.make_async_remote_copy(
            src_ref=source, dst_ref=target, send_sem=send_sem.at[kind, chunk], recv_sem=recv_sem.at[kind, chunk],
            device_id={"seq": device}, device_id_type=MESH,
        )

    def heads(chunk):
        return pl.ds(chunk * HC, HC)

    def cols(head, count=1):
        return pl.ds(head * E, count * E)

    links = {}
    for c in range(NC):
        links[S1, c] = push(S1, c, memory.at[0, heads(c)], memory.at[2, heads(c)], chip_at(1))
        links[S2, c] = push(S2, c, memory.at[0, heads(c)], memory.at[4, heads(c)], chip_at(2))
        links[R1, c] = push(R1, c, memory.at[2 * core, heads(c)], memory.at[1, heads(c)], twin)
        links[R3, c] = push(R3, c, memory.at[2 + 2 * core, heads(c)], memory.at[3, heads(c)], twin)
        links[T1, c] = push(T1, c, slot_grads.at[0, heads(c)], sibling.at[1 - core, heads(c)], twin)
        links[T3, c] = push(T3, c, slot_grads.at[2, heads(c)], sibling.at[2 - core, heads(c)], twin)
        links[U1, c] = push(U1, c, totals.at[0, heads(c)], arrived.at[0, heads(c)], chip_at(-1))
        links[U2, c] = push(U2, c, totals.at[1, heads(c)], arrived.at[1, heads(c)], chip_at(-2))

    sibling[2 - 2 * core] = jnp.zeros((H, 2 * ROWS, E), BF)

    row = lax.broadcasted_iota(jnp.int32, (SEG, SEG), 0)
    col = lax.broadcasted_iota(jnp.int32, (SEG, SEG), 1)
    row_key = 4 * (row % ROWS) + row // ROWS
    col_key = 4 * (col % ROWS) + col // ROWS
    perms[0] = jnp.where(col == row_key, 1.0, 0.0).astype(BF)
    perms[1] = jnp.where(row == col_key, 1.0, 0.0).astype(BF)
    slot = row // ROWS + 1
    seen = jnp.minimum(reach[0, 0], me)
    bias[0:SEG] = jnp.where(slot <= seen, 0.0, -1e30)
    bias[SEG:] = jnp.where(row_key <= col, 0.0, -1e30)

    def compress(c):
        span = cols(c * HC, HC)
        rows = []
        for source, target in ((k_in, k_perm), (v_in, v_perm)):
            moved = nn(perms[0], source[:, span]).astype(BF)
            for h in range(HC):
                one = moved[:, h * E:(h + 1) * E]
                target[c * HC + h] = one
                rows.append(jnp.concatenate([one[t * ROWS:(t + 1) * ROWS] for t in range(4)], axis=1))
        lhs = jnp.concatenate(rows, axis=0)
        stacked[c] = lhs
        packed = nn(lhs, w_in[...]).astype(BF)
        for h in range(HC):
            memory[0, c * HC + h, 0:ROWS] = packed[h * ROWS:(h + 1) * ROWS]
            memory[0, c * HC + h, ROWS:] = packed[(HC + h) * ROWS:(HC + h + 1) * ROWS]

    def attend(h):
        keys = jnp.concatenate([memory[r, h, 0:ROWS] for r in range(1, 5)] + [k_perm[h]], axis=0)
        values = jnp.concatenate([memory[r, h, ROWS:] for r in range(1, 5)] + [v_perm[h]], axis=0)
        query = q_in[:, cols(h)]
        grad = g_in[:, cols(h)]
        scores = nt(keys, query) * (SCALE * LOG2E) + bias[...]
        raised = jnp.exp2(scores - jnp.max(scores, axis=0, keepdims=True))
        weights = raised * (1.0 / jnp.sum(raised, axis=0, keepdims=True))
        low = weights.astype(BF)
        grad_weights = nt(values, grad)
        delta = jnp.sum(weights * grad_weights, axis=0, keepdims=True)
        grad_scores = (weights * (grad_weights - delta) * SCALE).astype(BF)
        att_out[:, cols(h)] = tn(low, values).astype(BF)
        gq_out[:, cols(h)] = tn(grad_scores, keys).astype(BF)
        for i, terms in enumerate((nn(grad_scores, query), nn(low, grad))):
            own[i, h] = terms[SEG:]
            for r in range(SLOTS):
                slot_grads[r, h, i * ROWS:(i + 1) * ROWS] = terms[r * ROWS:(r + 1) * ROWS].astype(BF)

    def combine(c):
        links[T1, c].wait_recv()
        links[T3, c].wait_recv()
        for i in range(2):
            totals[i, heads(c)] = (
                slot_grads[2 * i + 1, heads(c)].astype(F32) + sibling[i + 1, heads(c)].astype(F32)
            ).astype(BF)
        links[U1, c].start()
        links[U2, c].start()

    def finish(c, kernel_terms):
        links[U1, c].wait_recv()
        links[U2, c].wait_recv()
        memory_grads = (
            arrived[0, heads(c)].astype(F32) + arrived[1, heads(c)].astype(F32) + sibling[0, heads(c)].astype(F32)
        ).astype(BF)
        rows = jnp.concatenate(
            [memory_grads[h, i * ROWS:(i + 1) * ROWS] for i in range(2) for h in range(HC)], axis=0
        )
        terms = tn(stacked[c], rows)
        back = nt(rows, w_in[...])
        for i, out in enumerate((gk_out, gv_out)):
            pieces = []
            for h in range(HC):
                first = (i * HC + h) * ROWS
                spread = jnp.concatenate(
                    [back[first:first + ROWS, t * E:(t + 1) * E] for t in range(4)], axis=0
                )
                pieces.append((own[i, c * HC + h] + spread).astype(BF))
            out[:, cols(c * HC, HC)] = nn(perms[1], jnp.concatenate(pieces, axis=1)).astype(BF)
        return terms if kernel_terms is None else kernel_terms + terms

    for load in loads[:3]:
        load.wait()
    for c in range(NC):
        compress(c)
        if c == 0:
            pl.semaphore_wait(barrier, chips + books - 1)
        links[S1, c].start()
        links[S2, c].start()
    for load in loads[3:]:
        load.wait()

    kernel_terms = None
    def relay(c):
        links[S1, c].wait_recv()
        links[S2, c].wait_recv()
        links[R1, c].start()
        links[R3, c].start()

    relay(0)
    for c in range(NC):
        if c + 1 < NC:
            relay(c + 1)
        links[R1, c].wait_recv()
        links[R3, c].wait_recv()
        for h in range(HC):
            attend(c * HC + h)
        links[T1, c].start()
        links[T3, c].start()
        if c >= 1:
            combine(c - 1)
        if c >= 2:
            kernel_terms = finish(c - 2, kernel_terms)
    combine(NC - 1)
    for c in range(max(NC - 2, 0), NC):
        kernel_terms = finish(c, kernel_terms)

    share = 4 * E // (2 * chips)
    for i in range(2 * chips):
        kg_half[i % 2, i // 2] = kernel_terms[i * share:(i + 1) * share]
    swap = pltpu.make_async_remote_copy(
        src_ref=kg_half.at[1 - core], dst_ref=kg_pair, send_sem=ring_send.at[0], recv_sem=ring_recv.at[0],
        device_id={"seq": twin}, device_id_type=MESH,
    )
    swap.start()
    swap.wait_recv()
    kg_sent[...] = (kg_half[core] + kg_pair[...]).astype(BF)
    around = []
    for step in range(1, chips):
        around.append(pltpu.make_async_remote_copy(
            src_ref=kg_sent.at[(chip + step) % chips], dst_ref=kg_got.at[step],
            send_sem=ring_send.at[step], recv_sem=ring_recv.at[step],
            device_id={"seq": chip_at(step)}, device_id_type=MESH,
        ))
    for copy in around:
        copy.start()
    total = kg_sent[chip].astype(F32)
    for step, copy in enumerate(around):
        copy.wait_recv()
        total = total + kg_got[step + 1].astype(F32)
    kg_books[book] = total
    across = []
    for step in range(1, books):
        across.append(pltpu.make_async_remote_copy(
            src_ref=kg_books.at[book], dst_ref=kg_books.at[book],
            send_sem=book_send.at[step], recv_sem=book_recv.at[step],
            device_id={"dp": (book + step) % books}, device_id_type=MESH,
        ))
    for copy in across:
        copy.start()
    for copy in across:
        copy.wait_recv()
    whole = kg_books[0]
    for i in range(1, books):
        whole = whole + kg_books[i]
    gw_out[...] = whole
    for c in range(NC):
        for kind in range(8):
            links[kind, c].wait_send()
    swap.wait_send()
    for copy in around + across:
        copy.wait_send()


def store_kernel(*refs):
    count = (len(refs) - 1) // 2
    copies = [pltpu.make_async_copy(refs[i], refs[count + i], refs[-1].at[i]) for i in range(count)]
    for copy in copies:
        copy.start()
    for copy in copies:
        copy.wait()


def solution(mesh):
    chips = mesh.shape["seq"] // 2
    books = mesh.shape["dp"]

    def local(queries, key_vectors, value_vectors, cotangent, compress_kernel, memory_reach):
        share = 4 * E // (2 * chips)
        shapes = [((SEG, WIDTH), BF)] * 4 + [((share, E), F32)]
        anywhere = pl.BlockSpec(memory_space=pl.ANY)
        local_memory = pl.BlockSpec(memory_space=pltpu.VMEM)
        vm = pltpu.VMEM
        results = pl.pallas_call(
            functools.partial(kernel, chips, books),
            out_shape=tuple(vm(shape, kind) for shape, kind in shapes),
            in_specs=[anywhere] * 5 + [pl.BlockSpec(memory_space=pltpu.SMEM)],
            out_specs=[local_memory] * 5,
            scratch_shapes=[
                *[vm((SEG, WIDTH), BF)] * 4, vm((4 * E, E), BF),
                vm((H, SEG, E), BF), vm((H, SEG, E), BF), vm((NC, 2 * HC * ROWS, 4 * E), BF),
                vm((5, H, 2 * ROWS, E), BF), vm((2 * SEG, SEG), F32), vm((2, SEG, SEG), BF),
                vm((SLOTS, H, 2 * ROWS, E), BF), vm((3, H, 2 * ROWS, E), BF), vm((2, H, 2 * ROWS, E), BF),
                vm((2, H, 2 * ROWS, E), BF), vm((2, H, SEG, E), F32),
                vm((2, chips, share, E), F32), vm((chips, share, E), F32), vm((chips, share, E), BF),
                vm((chips, share, E), BF), vm((books, share, E), F32),
                pltpu.SemaphoreType.DMA((5,)),
                pltpu.SemaphoreType.DMA((8, NC)), pltpu.SemaphoreType.DMA((8, NC)),
                pltpu.SemaphoreType.DMA((chips,)), pltpu.SemaphoreType.DMA((chips,)),
                pltpu.SemaphoreType.DMA((books,)), pltpu.SemaphoreType.DMA((books,)),
            ],
            compiler_params=pltpu.CompilerParams(collective_id=0, has_side_effects=True),
        )(queries, key_vectors, value_vectors, cotangent, compress_kernel, memory_reach)
        results = [pltpu.with_memory_space_constraint(result, pltpu.VMEM) for result in results]
        stored = pl.pallas_call(
            store_kernel,
            out_shape=tuple(jax.ShapeDtypeStruct(shape, kind) for shape, kind in shapes),
            in_specs=[local_memory] * 5,
            out_specs=[anywhere] * 5,
            scratch_shapes=[pltpu.SemaphoreType.DMA((5,))],
        )(*results)
        return tuple(whole[None] for whole in stored[:4]) + (stored[4],)

    rows = P("dp", "seq", None)
    return jax.shard_map(
        local, mesh=mesh, in_specs=(rows, rows, rows, rows, P(), P("dp", "seq")),
        out_specs=(rows, rows, rows, rows, P("seq", None)), check_vma=False,
    )
```

```python
import functools

import jax
import jax.numpy as jnp
from jax import lax
from jax.experimental import pallas as pl
from jax.experimental.pallas import tpu as pltpu
from jax.sharding import PartitionSpec as P

MESH = pl.DeviceIdType.MESH
H = 16
E = 128
SEG = 128
ROWS = SEG // 4
SLOTS = 4
HALF = H // 2
SIZES = (2, 2, 2, 2)
NC = len(SIZES)
FIRST = tuple(sum(SIZES[:c]) for c in range(NC))
FORWARD = (0, 1, 2, 3)
BACKWARD = (0, 1)
LAG = 1
WIDTH = H * E
SPAN = HALF * E
BF = jnp.bfloat16
F32 = jnp.float32
SCALE = E ** -0.5
LOG2E = 1.4426950408889634
S1, S2, F, U1, U2, KINDS = 0, 2, 4, 5, 6, 7
XP, XD, XQ, XG, XB, XO, SWAPS = 0, 1, 2, 3, 4, 5, 9


def nn(a, b):
    return lax.dot_general(a, b, (((1,), (0,)), ((), ())), preferred_element_type=F32)


def nt(a, b):
    return lax.dot_general(a, b, (((1,), (1,)), ((), ())), preferred_element_type=F32)


def tn(a, b):
    return lax.dot_general(a, b, (((0,), (0,)), ((), ())), preferred_element_type=F32)


def kernel(
    chips, books,
    q_hbm, k_hbm, v_hbm, g_hbm, w_hbm, reach,
    att_out, gq_out, gk_out, gv_out, gw_out,
    k_in, v_in, w_in, perms, perm, packed, memory, segments, sides, bias,
    totals, local, arrived, own, kept, summed, results,
    kg_half, kg_pair, kg_sent, kg_got, kg_books,
    load_sem, send_sem, recv_sem, swap_send, swap_recv, swap_local,
    ring_send, ring_recv, book_send, book_recv,
):
    me = lax.axis_index("seq")
    book = lax.axis_index("dp")
    chip = me // 2
    core = me % 2
    side = chip % 2
    twin = me + 1 - 2 * core

    def chip_at(step):
        return (chip + step + chips) % chips

    def seat(step):
        return chip_at(step) * 2 + core

    def half(which):
        return pl.ds(pl.multiple_of(which * SPAN, SPAN), SPAN)

    loads = [
        pltpu.make_async_copy(source, target, load_sem.at[i])
        for i, (source, target) in enumerate([(k_hbm.at[0], k_in), (v_hbm.at[0], v_in), (w_hbm, w_in)])
    ]
    for load in loads:
        load.start()

    barrier = pltpu.get_barrier_semaphore()

    def greet(**where):
        pl.semaphore_signal(barrier, inc=1, device_id=where, device_id_type=MESH)

    greet(seq=twin)
    for step in range(1, chips):
        greet(seq=seat(step))
    for step in range(1, 3):
        greet(seq=chip_at(step) * 2 + 1 - core)
        greet(seq=chip_at(-step) * 2 + 1 - core)
    for step in range(1, books):
        greet(dp=(book + step) % books)

    def heads(chunk, which=0):
        return pl.ds(which * HALF + FIRST[chunk], SIZES[chunk])

    def cols(head, count=1):
        return pl.ds(head * E, count * E)

    def push(source, target, sent, got, device):
        return pltpu.make_async_remote_copy(
            src_ref=source, dst_ref=target, send_sem=sent, recv_sem=got,
            device_id={"seq": device}, device_id_type=MESH,
        )

    def rows(c, first, count):
        return memory.at[heads(c), :, pl.ds(first, count)]

    own_row = pl.multiple_of(ROWS * core, ROWS)
    links = {}
    for c in range(NC):
        for j in range(2):
            links[S1 + j, c] = push(
                packed.at[heads(c, j)], rows(c, 2 * ROWS + own_row, ROWS),
                send_sem.at[S1 + j, c], recv_sem.at[S1 + core, c], chip_at(1) * 2 + j,
            )
            links[S2 + j, c] = push(
                packed.at[heads(c, j)], rows(c, own_row, ROWS),
                send_sem.at[S2 + j, c], recv_sem.at[S2 + core, c], chip_at(2) * 2 + j,
            )
        links[F, c] = push(
            rows(c, 0, 2 * ROWS), rows(c, 2 * ROWS, 2 * ROWS), send_sem.at[F, c], recv_sem.at[F, c], seat(-1),
        )
        links[U1, c] = push(
            totals.at[heads(c), :, pl.ds(2 * ROWS, 2 * ROWS)], arrived.at[0, heads(c)],
            send_sem.at[U1, c], recv_sem.at[U1, c], seat(1 - 2 * side) if c in BACKWARD else seat(-1),
        )
        links[U2, c] = push(
            totals.at[heads(c), :, pl.ds(0, 2 * ROWS)], arrived.at[1, heads(c)],
            send_sem.at[U2, c], recv_sem.at[U2, c], seat(-2),
        )

    def landed(kind, c):
        for k in range(2):
            push(
                packed.at[heads(c)], rows(c, 2 * ROWS if kind == S1 else 0, ROWS),
                send_sem.at[kind + k, c], recv_sem.at[kind + k, c], twin,
            ).wait_recv()

    def swap_pair(kind, mine, other, here, there):
        return (
            pltpu.make_async_copy(mine, here, swap_local.at[kind]),
            push(other, there, swap_send.at[kind], swap_recv.at[kind], twin),
        )

    def half_heads(which):
        return pl.ds(which * HALF, HALF)

    mid_rows = memory.at[:, :, pl.ds(4 * ROWS + own_row, ROWS)]
    swaps = {
        XP: swap_pair(XP, perm.at[half_heads(core)], perm.at[half_heads(1 - core)], segments.at[core], segments.at[core]),
        XD: swap_pair(XD, packed.at[half_heads(core)], packed.at[half_heads(1 - core)], mid_rows, mid_rows),
    }
    for kind, source in ((XQ, q_hbm), (XG, g_hbm)):
        target = sides.at[core, kind - XQ]
        swaps[kind] = swap_pair(kind, source.at[0, :, half(core)], source.at[0, :, half(1 - core)], target, target)
    for i, out in enumerate((att_out, gq_out, gk_out, gv_out)):
        target = out.at[:, half(core)]
        swaps[XO + i] = swap_pair(XO + i, results.at[i, core], results.at[i, 1 - core], target, target)
    open_rows = bias.at[core, pl.ds(0, SEG)]
    bias_swap = push(open_rows, open_rows, swap_send.at[XB], swap_recv.at[XB], twin)

    def hand_out(i):
        for copy in swaps[XO + i]:
            copy.start()

    swaps[XQ][0].start()
    swaps[XG][0].start()

    row = lax.broadcasted_iota(jnp.int32, (SEG, SEG), 0)
    col = lax.broadcasted_iota(jnp.int32, (SEG, SEG), 1)
    row_key = 4 * (row % ROWS) + row // ROWS
    col_key = 4 * (col % ROWS) + col // ROWS
    perms[0] = jnp.where(col == row_key, 1.0, 0.0).astype(BF)
    perms[1] = jnp.where(row == col_key, 1.0, 0.0).astype(BF)
    seen = jnp.minimum(reach[0, 0], me)
    bias[core, 0:SEG] = jnp.where(SLOTS - row // ROWS <= seen, 0.0, -1e30)
    causal = jnp.where(row_key <= col, 0.0, -1e30)
    bias[0, SEG:] = causal
    bias[1, SEG:] = causal

    def spread_lanes(one):
        return jnp.concatenate([one[t * ROWS:(t + 1) * ROWS] for t in range(4)], axis=1)

    def compress(c):
        size = SIZES[c]
        lhs, places = [], []
        for j in range(2):
            first = j * HALF + FIRST[c]
            for i, source in enumerate((k_in, v_in)):
                moved = nn(perms[0], source[:, cols(first, size)]).astype(BF)
                for h in range(size):
                    one = moved[:, h * E:(h + 1) * E]
                    perm[first + h, i] = one
                    lhs.append(spread_lanes(one))
                    places.append((first + h, i))
        out = nn(jnp.concatenate(lhs, axis=0), w_in[...]).astype(BF)
        for n, (h, i) in enumerate(places):
            packed[h, i] = out[n * ROWS:(n + 1) * ROWS]

    def listed(p, h, i):
        return jnp.concatenate([memory[h, i, p * ROWS:p * ROWS + SEG], segments[p, h, i]], axis=0)

    def score(h):
        pieces = []
        for p in range(2):
            query = sides[p, 0, :, cols(h)]
            grad = sides[p, 1, :, cols(h)]
            scores = nt(listed(p, h, 0), query) * (SCALE * LOG2E) + bias[p]
            raised = jnp.exp2(scores - jnp.max(scores, axis=0, keepdims=True))
            weights = raised * (1.0 / jnp.sum(raised, axis=0, keepdims=True))
            low = weights.astype(BF)
            grad_weights = nt(listed(p, h, 1), grad)
            delta = jnp.sum(weights * grad_weights, axis=0, keepdims=True)
            grad_scores = (weights * (grad_weights - delta) * SCALE).astype(BF)
            kept[p, 0, h] = grad_scores
            kept[p, 1, h] = low
            pieces.append((nn(grad_scores[:SEG], query), nn(low[:SEG], grad)))
        for i in range(2):
            left, right = pieces[0][i], pieces[1][i]
            totals[h, i, 0:ROWS] = left[:ROWS].astype(BF)
            totals[h, i, ROWS:] = (left[ROWS:] + right[:SEG - ROWS]).astype(BF)
            local[h, i] = right[SEG - ROWS:]

    def attend(h):
        for p in range(2):
            grad_scores, low = kept[p, 0, h], kept[p, 1, h]
            results[0, p, :, cols(h)] = tn(low, listed(p, h, 1)).astype(BF)
            results[1, p, :, cols(h)] = tn(grad_scores, listed(p, h, 0)).astype(BF)
            own[0, p, h] = nn(grad_scores[SEG:], sides[p, 0, :, cols(h)])
            own[1, p, h] = nn(low[SEG:], sides[p, 1, :, cols(h)])

    def combine(c):
        links[U1, c].start()
        if c in BACKWARD:
            pl.when(side == 0)(links[U2, c].start)
        else:
            links[U2, c].start()

    def carry(c):
        if c in BACKWARD:
            links[U1, c].wait_recv()

            @pl.when(side == 1)
            def _():
                totals[heads(c), :, 0:2 * ROWS] = (
                    totals[heads(c), :, 0:2 * ROWS].astype(F32) + arrived[0, heads(c)].astype(F32)
                ).astype(BF)
                links[U2, c].start()

    def chunk_heads(c):
        return range(FIRST[c], FIRST[c] + SIZES[c])

    def gather(c):
        if c not in BACKWARD:
            links[U1, c].wait_recv()
        links[U2, c].wait_recv()
        lhs, rhs = [], []
        for h in chunk_heads(c):
            near = arrived[0, h].astype(F32)
            if c in BACKWARD:
                near = jnp.where(side == 0, near, 0.0)
            whole = near + arrived[1, h].astype(F32)
            for i in range(2):
                one = jnp.concatenate([whole[i, :ROWS] + local[h, i], whole[i, ROWS:]], axis=0).astype(BF)
                summed[h, i] = one
                rhs.append(one)
                for p in range(2):
                    lhs.append(spread_lanes(segments[p, h, i]))
        return tn(jnp.concatenate(lhs, axis=0), jnp.concatenate(rhs, axis=0))

    def finish(c):
        size = SIZES[c]
        back = nt(jnp.concatenate([summed[h, i] for h in chunk_heads(c) for i in range(2)], axis=0), w_in[...])
        for i in range(2):
            for p in range(2):
                pieces = []
                for n, h in enumerate(chunk_heads(c)):
                    start = (4 * n + 2 * i + p) * ROWS
                    wide = jnp.concatenate(
                        [back[start:start + ROWS, t * E:(t + 1) * E] for t in range(4)], axis=0
                    )
                    pieces.append((own[i, p, h] + wide).astype(BF))
                results[2 + i, p, :, cols(FIRST[c], size)] = nn(
                    perms[1], jnp.concatenate(pieces, axis=1)
                ).astype(BF)

    def pass_on(c):
        if c in FORWARD:
            landed(S2, c)
            pl.when(side == 1)(links[F, c].start)

    def ready(c):
        if c in FORWARD:
            pl.when(side == 1)(lambda: landed(S1, c))
            pl.when(side == 0)(links[F, c].wait_recv)
        else:
            landed(S2, c)
            landed(S1, c)

    def send(c):
        for j in range(2):
            links[S2 + j, c].start()
        for j in range(2):
            if c in FORWARD:
                pl.when(side == 0)(links[S1 + j, c].start)
            else:
                links[S1 + j, c].start()

    for load in loads:
        load.wait()
    for c in range(NC):
        compress(c)
    pl.semaphore_wait(barrier, chips + books + 3)
    for c in range(NC):
        send(c)
    for kind in (XP, XD):
        for copy in swaps[kind]:
            copy.start()
    bias_swap.start()
    swaps[XQ][1].start()
    swaps[XG][1].start()
    for kind in (XP, XD, XQ, XG):
        swaps[kind][0].wait()
        swaps[kind][1].wait_recv()
    bias_swap.wait_recv()

    pass_on(0)
    pass_on(1)
    for c in range(NC):
        if c + 2 < NC:
            pass_on(c + 2)
        ready(c)
        for h in chunk_heads(c):
            score(h)
        combine(c)
        for h in chunk_heads(c):
            attend(h)
        if c >= LAG:
            carry(c - LAG)
    hand_out(0)
    hand_out(1)
    for c in range(NC - LAG, NC):
        carry(c)
    kernel_terms = gather(0)
    finish(0)
    for c in range(1, NC):
        kernel_terms = kernel_terms + gather(c)
        if c + 2 < NC:
            finish(c)

    share = 4 * E // (2 * chips)
    for i in range(2 * chips):
        kg_half[i % 2, i // 2] = kernel_terms[i * share:(i + 1) * share]
    swap = pltpu.make_async_remote_copy(
        src_ref=kg_half.at[1 - core], dst_ref=kg_pair, send_sem=ring_send.at[0], recv_sem=ring_recv.at[0],
        device_id={"seq": twin}, device_id_type=MESH,
    )
    swap.start()
    finish(NC - 2)
    swap.wait_recv()
    kg_sent[...] = (kg_half[core] + kg_pair[...]).astype(BF)
    around = []
    for step in range(1, chips):
        around.append(pltpu.make_async_remote_copy(
            src_ref=kg_sent.at[(chip + step) % chips], dst_ref=kg_got.at[step],
            send_sem=ring_send.at[step], recv_sem=ring_recv.at[step],
            device_id={"seq": seat(step)}, device_id_type=MESH,
        ))
    for copy in around:
        copy.start()
    finish(NC - 1)
    hand_out(2)
    hand_out(3)
    total = kg_sent[chip].astype(F32)
    for step, copy in enumerate(around):
        copy.wait_recv()
        total = total + kg_got[step + 1].astype(F32)
    kg_books[book] = total
    across = []
    for step in range(1, books):
        across.append(pltpu.make_async_remote_copy(
            src_ref=kg_books.at[book], dst_ref=kg_books.at[book],
            send_sem=book_send.at[step], recv_sem=book_recv.at[step],
            device_id={"dp": (book + step) % books}, device_id_type=MESH,
        ))
    for copy in across:
        copy.start()
    for copy in across:
        copy.wait_recv()
    whole = kg_books[0]
    for i in range(1, books):
        whole = whole + kg_books[i]
    gw_out[...] = whole
    for c in range(NC):
        for kind in (S2, S2 + 1, U1, U2):
            links[kind, c].wait_send()
        if c in FORWARD:
            pl.when(side == 1)(links[F, c].wait_send)
        for j in range(2):
            if c in FORWARD:
                pl.when(side == 0)(links[S1 + j, c].wait_send)
            else:
                links[S1 + j, c].wait_send()
    for kind in (XP, XD, XQ, XG):
        swaps[kind][1].wait_send()
    bias_swap.wait_send()
    for i in range(4):
        swaps[XO + i][0].wait()
        swaps[XO + i][1].wait()
    swap.wait_send()
    for copy in around + across:
        copy.wait_send()


def store_kernel(*refs):
    count = (len(refs) - 1) // 2
    copies = [pltpu.make_async_copy(refs[i], refs[count + i], refs[-1].at[i]) for i in range(count)]
    for copy in copies:
        copy.start()
    for copy in copies:
        copy.wait()


def solution(mesh):
    chips = mesh.shape["seq"] // 2
    books = mesh.shape["dp"]

    def local(queries, key_vectors, value_vectors, cotangent, compress_kernel, memory_reach):
        share = 4 * E // (2 * chips)
        shapes = [((SEG, WIDTH), BF)] * 4 + [((share, E), F32)]
        anywhere = pl.BlockSpec(memory_space=pl.ANY)
        local_memory = pl.BlockSpec(memory_space=pltpu.VMEM)
        vm = pltpu.VMEM
        results = pl.pallas_call(
            functools.partial(kernel, chips, books),
            out_shape=tuple(vm(shape, kind) for shape, kind in shapes),
            in_specs=[anywhere] * 5 + [pl.BlockSpec(memory_space=pltpu.SMEM)],
            out_specs=[local_memory] * 5,
            scratch_shapes=[
                vm((SEG, WIDTH), BF), vm((SEG, WIDTH), BF), vm((4 * E, E), BF), vm((2, SEG, SEG), BF),
                vm((H, 2, SEG, E), BF), vm((H, 2, ROWS, E), BF), vm((HALF, 2, 6 * ROWS, E), BF),
                vm((2, HALF, 2, SEG, E), BF), vm((2, 2, SEG, SPAN), BF), vm((2, 2 * SEG, SEG), F32),
                vm((HALF, 2, SEG, E), BF), vm((HALF, 2, ROWS, E), F32), vm((2, HALF, 2, 2 * ROWS, E), BF),
                vm((2, 2, HALF, SEG, E), F32), vm((2, 2, HALF, 2 * SEG, SEG), BF),
                vm((HALF, 2, 2 * ROWS, E), BF), vm((4, 2, SEG, SPAN), BF),
                vm((2, chips, share, E), F32), vm((chips, share, E), F32), vm((chips, share, E), BF),
                vm((chips, share, E), BF), vm((books, share, E), F32),
                pltpu.SemaphoreType.DMA((3,)),
                pltpu.SemaphoreType.DMA((KINDS, NC)), pltpu.SemaphoreType.DMA((KINDS, NC)),
                pltpu.SemaphoreType.DMA((SWAPS,)), pltpu.SemaphoreType.DMA((SWAPS,)), pltpu.SemaphoreType.DMA((SWAPS,)),
                pltpu.SemaphoreType.DMA((chips,)), pltpu.SemaphoreType.DMA((chips,)),
                pltpu.SemaphoreType.DMA((books,)), pltpu.SemaphoreType.DMA((books,)),
            ],
            compiler_params=pltpu.CompilerParams(collective_id=0, has_side_effects=True),
        )(queries, key_vectors, value_vectors, cotangent, compress_kernel, memory_reach)
        results = [pltpu.with_memory_space_constraint(result, pltpu.VMEM) for result in results]
        stored = pl.pallas_call(
            store_kernel,
            out_shape=tuple(jax.ShapeDtypeStruct(shape, kind) for shape, kind in shapes),
            in_specs=[local_memory] * 5,
            out_specs=[anywhere] * 5,
            scratch_shapes=[pltpu.SemaphoreType.DMA((5,))],
        )(*results)
        return tuple(whole[None] for whole in stored[:4]) + (stored[4],)

    rows = P("dp", "seq", None)
    return jax.shard_map(
        local, mesh=mesh, in_specs=(rows, rows, rows, rows, P(), P("dp", "seq")),
        out_specs=(rows, rows, rows, rows, P("seq", None)), check_vma=False,
    )
```

```python
import functools

import jax
import jax.numpy as jnp
from jax import lax
from jax.experimental import pallas as pl
from jax.experimental.pallas import tpu as pltpu
from jax.sharding import PartitionSpec as P

MESH = pl.DeviceIdType.MESH
H = 16
E = 128
SEG = 128
ROWS = SEG // 4
SLOTS = 4
HALF = H // 2
SIZES = (1,) * HALF
NC = len(SIZES)
FIRST = tuple(sum(SIZES[:c]) for c in range(NC))
FORWARD = ()
BACKWARD = ()
LAG = 1
WIDTH = H * E
SPAN = HALF * E
BF = jnp.bfloat16
F32 = jnp.float32
SCALE = E ** -0.5
LOG2E = 1.4426950408889634
S1, S2, F, U1, U2, KINDS = 0, 2, 4, 5, 6, 7
XP, XD, XQ, XG, XB, XO, SWAPS = 0, 1, 2, 3, 4, 5, 9


def nn(a, b):
    return lax.dot_general(a, b, (((1,), (0,)), ((), ())), preferred_element_type=F32)


def nt(a, b):
    return lax.dot_general(a, b, (((1,), (1,)), ((), ())), preferred_element_type=F32)


def tn(a, b):
    return lax.dot_general(a, b, (((0,), (0,)), ((), ())), preferred_element_type=F32)


def kernel(
    chips, books,
    q_hbm, k_hbm, v_hbm, g_hbm, w_hbm, reach,
    att_out, gq_out, gk_out, gv_out, gw_out,
    k_in, v_in, w_in, perms, perm, packed, memory, segments, sides, bias,
    totals, local, arrived, own, kept, summed, results,
    kg_half, kg_pair, kg_sent, kg_got, kg_books,
    load_sem, send_sem, recv_sem, swap_send, swap_recv, swap_local,
    ring_send, ring_recv, book_send, book_recv,
):
    me = lax.axis_index("seq")
    book = lax.axis_index("dp")
    chip = me // 2
    core = me % 2
    side = chip % 2
    twin = me + 1 - 2 * core

    def chip_at(step):
        return (chip + step + chips) % chips

    def seat(step):
        return chip_at(step) * 2 + core

    def half(which):
        return pl.ds(pl.multiple_of(which * SPAN, SPAN), SPAN)

    loads = [
        pltpu.make_async_copy(source, target, load_sem.at[i])
        for i, (source, target) in enumerate([(k_hbm.at[0], k_in), (v_hbm.at[0], v_in), (w_hbm, w_in)])
    ]
    barrier = pltpu.get_barrier_semaphore()

    def greet(**where):
        pl.semaphore_signal(barrier, inc=1, device_id=where, device_id_type=MESH)

    for step in range(books - 1, 0, -1):
        greet(dp=(book + step) % books)
    for step in sorted(range(1, chips), key=lambda one: -min(one, chips - one)):
        greet(seq=seat(step))
    for step in range(1, 3):
        greet(seq=chip_at(step) * 2 + 1 - core)
        greet(seq=chip_at(-step) * 2 + 1 - core)
    greet(seq=twin)
    for load in loads:
        load.start()

    def heads(chunk, which=0):
        return pl.ds(which * HALF + FIRST[chunk], SIZES[chunk])

    def cols(head, count=1):
        return pl.ds(head * E, count * E)

    def push(source, target, sent, got, device):
        return pltpu.make_async_remote_copy(
            src_ref=source, dst_ref=target, send_sem=sent, recv_sem=got,
            device_id={"seq": device}, device_id_type=MESH,
        )

    def rows(c, first, count):
        return memory.at[heads(c), :, pl.ds(first, count)]

    own_row = pl.multiple_of(ROWS * core, ROWS)
    links = {}
    for c in range(NC):
        for j in range(2):
            links[S1 + j, c] = push(
                packed.at[heads(c, j)], rows(c, 2 * ROWS + own_row, ROWS),
                send_sem.at[S1 + j, c], recv_sem.at[S1 + core, c], chip_at(1) * 2 + j,
            )
            links[S2 + j, c] = push(
                packed.at[heads(c, j)], rows(c, own_row, ROWS),
                send_sem.at[S2 + j, c], recv_sem.at[S2 + core, c], chip_at(2) * 2 + j,
            )
        links[F, c] = push(
            rows(c, 0, 2 * ROWS), rows(c, 2 * ROWS, 2 * ROWS), send_sem.at[F, c], recv_sem.at[F, c], seat(-1),
        )
        links[U1, c] = push(
            totals.at[heads(c), :, pl.ds(2 * ROWS, 2 * ROWS)], arrived.at[0, heads(c)],
            send_sem.at[U1, c], recv_sem.at[U1, c], seat(1 - 2 * side) if c in BACKWARD else seat(-1),
        )
        links[U2, c] = push(
            totals.at[heads(c), :, pl.ds(0, 2 * ROWS)], arrived.at[1, heads(c)],
            send_sem.at[U2, c], recv_sem.at[U2, c], seat(-2),
        )

    def landed(kind, c):
        for k in range(2):
            push(
                packed.at[heads(c)], rows(c, 2 * ROWS if kind == S1 else 0, ROWS),
                send_sem.at[kind + k, c], recv_sem.at[kind + k, c], twin,
            ).wait_recv()

    def swap_pair(kind, mine, other, here, there):
        return (
            pltpu.make_async_copy(mine, here, swap_local.at[kind]),
            push(other, there, swap_send.at[kind], swap_recv.at[kind], twin),
        )

    def half_heads(which):
        return pl.ds(which * HALF, HALF)

    mid_rows = memory.at[:, :, pl.ds(4 * ROWS + own_row, ROWS)]
    swaps = {
        XP: swap_pair(XP, perm.at[half_heads(core)], perm.at[half_heads(1 - core)], segments.at[core], segments.at[core]),
        XD: swap_pair(XD, packed.at[half_heads(core)], packed.at[half_heads(1 - core)], mid_rows, mid_rows),
    }
    for kind, source in ((XQ, q_hbm), (XG, g_hbm)):
        target = sides.at[core, kind - XQ]
        swaps[kind] = swap_pair(kind, source.at[0, :, half(core)], source.at[0, :, half(1 - core)], target, target)
    for i, out in enumerate((att_out, gq_out, gk_out, gv_out)):
        target = out.at[:, half(core)]
        swaps[XO + i] = swap_pair(XO + i, results.at[i, core], results.at[i, 1 - core], target, target)
    open_rows = bias.at[core, pl.ds(0, SEG)]
    bias_swap = push(open_rows, open_rows, swap_send.at[XB], swap_recv.at[XB], twin)

    def hand_out(i):
        for copy in swaps[XO + i]:
            copy.start()

    swaps[XQ][0].start()
    swaps[XG][0].start()

    row = lax.broadcasted_iota(jnp.int32, (SEG, SEG), 0)
    col = lax.broadcasted_iota(jnp.int32, (SEG, SEG), 1)
    row_key = 4 * (row % ROWS) + row // ROWS
    col_key = 4 * (col % ROWS) + col // ROWS
    perms[0] = jnp.where(col == row_key, 1.0, 0.0).astype(BF)
    perms[1] = jnp.where(row == col_key, 1.0, 0.0).astype(BF)
    seen = jnp.minimum(reach[0, 0], me)
    bias[core, 0:SEG] = jnp.where(SLOTS - row // ROWS <= seen, 0.0, -1e30)
    causal = jnp.where(row_key <= col, 0.0, -1e30)
    bias[0, SEG:] = causal
    bias[1, SEG:] = causal

    def spread_lanes(one):
        return jnp.concatenate([one[t * ROWS:(t + 1) * ROWS] for t in range(4)], axis=1)

    def compress(c):
        size = SIZES[c]
        lhs, places = [], []
        for j in range(2):
            first = j * HALF + FIRST[c]
            for i, source in enumerate((k_in, v_in)):
                moved = nn(perms[0], source[:, cols(first, size)]).astype(BF)
                for h in range(size):
                    one = moved[:, h * E:(h + 1) * E]
                    perm[first + h, i] = one
                    lhs.append(spread_lanes(one))
                    places.append((first + h, i))
        out = nn(jnp.concatenate(lhs, axis=0), w_in[...]).astype(BF)
        for n, (h, i) in enumerate(places):
            packed[h, i] = out[n * ROWS:(n + 1) * ROWS]

    def listed(p, h, i):
        return jnp.concatenate([memory[h, i, p * ROWS:p * ROWS + SEG], segments[p, h, i]], axis=0)

    def score(h):
        pieces = []
        for p in range(2):
            query = sides[p, 0, :, cols(h)]
            grad = sides[p, 1, :, cols(h)]
            scores = nt(listed(p, h, 0), query) * (SCALE * LOG2E) + bias[p]
            raised = jnp.exp2(scores - jnp.max(scores, axis=0, keepdims=True))
            weights = raised * (1.0 / jnp.sum(raised, axis=0, keepdims=True))
            low = weights.astype(BF)
            grad_weights = nt(listed(p, h, 1), grad)
            delta = jnp.sum(weights * grad_weights, axis=0, keepdims=True)
            grad_scores = (weights * (grad_weights - delta) * SCALE).astype(BF)
            kept[p, 0, h] = grad_scores
            kept[p, 1, h] = low
            pieces.append((nn(grad_scores[:SEG], query), nn(low[:SEG], grad)))
        for i in range(2):
            left, right = pieces[0][i], pieces[1][i]
            totals[h, i, 0:ROWS] = left[:ROWS].astype(BF)
            totals[h, i, ROWS:] = (left[ROWS:] + right[:SEG - ROWS]).astype(BF)
            local[h, i] = right[SEG - ROWS:]

    def attend(h):
        for p in range(2):
            grad_scores, low = kept[p, 0, h], kept[p, 1, h]
            results[0, p, :, cols(h)] = tn(low, listed(p, h, 1)).astype(BF)
            results[1, p, :, cols(h)] = tn(grad_scores, listed(p, h, 0)).astype(BF)
            own[0, p, h] = nn(grad_scores[SEG:], sides[p, 0, :, cols(h)])
            own[1, p, h] = nn(low[SEG:], sides[p, 1, :, cols(h)])

    def combine(c):
        links[U1, c].start()
        if c in BACKWARD:
            pl.when(side == 0)(links[U2, c].start)
        else:
            links[U2, c].start()

    def carry(c):
        if c in BACKWARD:
            links[U1, c].wait_recv()

            @pl.when(side == 1)
            def _():
                totals[heads(c), :, 0:2 * ROWS] = (
                    totals[heads(c), :, 0:2 * ROWS].astype(F32) + arrived[0, heads(c)].astype(F32)
                ).astype(BF)
                links[U2, c].start()

    def chunk_heads(c):
        return range(FIRST[c], FIRST[c] + SIZES[c])

    def gather(c):
        if c not in BACKWARD:
            links[U1, c].wait_recv()
        links[U2, c].wait_recv()
        lhs, rhs = [], []
        for h in chunk_heads(c):
            near = arrived[0, h].astype(F32)
            if c in BACKWARD:
                near = jnp.where(side == 0, near, 0.0)
            whole = near + arrived[1, h].astype(F32)
            for i in range(2):
                one = jnp.concatenate([whole[i, :ROWS] + local[h, i], whole[i, ROWS:]], axis=0).astype(BF)
                summed[h, i] = one
                rhs.append(one)
                for p in range(2):
                    lhs.append(spread_lanes(segments[p, h, i]))
        return tn(jnp.concatenate(lhs, axis=0), jnp.concatenate(rhs, axis=0))

    def finish(c):
        size = SIZES[c]
        back = nt(jnp.concatenate([summed[h, i] for h in chunk_heads(c) for i in range(2)], axis=0), w_in[...])
        for i in range(2):
            for p in range(2):
                pieces = []
                for n, h in enumerate(chunk_heads(c)):
                    start = (4 * n + 2 * i + p) * ROWS
                    wide = jnp.concatenate(
                        [back[start:start + ROWS, t * E:(t + 1) * E] for t in range(4)], axis=0
                    )
                    pieces.append((own[i, p, h] + wide).astype(BF))
                results[2 + i, p, :, cols(FIRST[c], size)] = nn(
                    perms[1], jnp.concatenate(pieces, axis=1)
                ).astype(BF)

    def pass_on(c):
        if c in FORWARD:
            landed(S2, c)
            pl.when(side == 1)(links[F, c].start)

    def ready(c):
        if c in FORWARD:
            pl.when(side == 1)(lambda: landed(S1, c))
            pl.when(side == 0)(links[F, c].wait_recv)
        else:
            landed(S2, c)
            landed(S1, c)

    def send(c):
        for j in range(2):
            links[S2 + j, c].start()
        for j in range(2):
            if c in FORWARD:
                pl.when(side == 0)(links[S1 + j, c].start)
            else:
                links[S1 + j, c].start()

    for load in loads:
        load.wait()
    for c in range(NC):
        compress(c)
        if c == 0:
            pl.semaphore_wait(barrier, chips + books + 3)
        send(c)
        if c == 2:
            for kind in (XQ, XG):
                swaps[kind][1].start()
            bias_swap.start()
    for copy in swaps[XD] + swaps[XP]:
        copy.start()

    pass_on(0)
    pass_on(1)
    for kind in (XP, XD, XQ, XG):
        swaps[kind][0].wait()
        swaps[kind][1].wait_recv()
    bias_swap.wait_recv()
    for c in range(NC):
        if c + 2 < NC:
            pass_on(c + 2)
        ready(c)
        for h in chunk_heads(c):
            score(h)
        combine(c)
        for h in chunk_heads(c):
            attend(h)
        if c >= LAG:
            carry(c - LAG)
    hand_out(0)
    hand_out(1)
    for c in range(NC - LAG, NC):
        carry(c)
    kernel_terms = gather(0)
    finish(0)
    for c in range(1, NC):
        kernel_terms = kernel_terms + gather(c)
        if c + 2 < NC:
            finish(c)

    share = 4 * E // (2 * chips)
    for i in range(2 * chips):
        kg_half[i % 2, i // 2] = kernel_terms[i * share:(i + 1) * share]
    swap = pltpu.make_async_remote_copy(
        src_ref=kg_half.at[1 - core], dst_ref=kg_pair, send_sem=ring_send.at[0], recv_sem=ring_recv.at[0],
        device_id={"seq": twin}, device_id_type=MESH,
    )
    swap.start()
    finish(NC - 2)
    swap.wait_recv()
    kg_sent[...] = (kg_half[core] + kg_pair[...]).astype(BF)
    around = []
    for step in range(1, chips):
        around.append(pltpu.make_async_remote_copy(
            src_ref=kg_sent.at[(chip + step) % chips], dst_ref=kg_got.at[step],
            send_sem=ring_send.at[step], recv_sem=ring_recv.at[step],
            device_id={"seq": seat(step)}, device_id_type=MESH,
        ))
    for copy in around:
        copy.start()
    finish(NC - 1)
    hand_out(2)
    hand_out(3)
    total = kg_sent[chip].astype(F32)
    for step, copy in enumerate(around):
        copy.wait_recv()
        total = total + kg_got[step + 1].astype(F32)
    kg_books[book] = total
    across = []
    for step in range(1, books):
        across.append(pltpu.make_async_remote_copy(
            src_ref=kg_books.at[book], dst_ref=kg_books.at[book],
            send_sem=book_send.at[step], recv_sem=book_recv.at[step],
            device_id={"dp": (book + step) % books}, device_id_type=MESH,
        ))
    for copy in across:
        copy.start()
    for copy in across:
        copy.wait_recv()
    whole = kg_books[0]
    for i in range(1, books):
        whole = whole + kg_books[i]
    gw_out[...] = whole
    for c in range(NC):
        for kind in (S2, S2 + 1, U1, U2):
            links[kind, c].wait_send()
        if c in FORWARD:
            pl.when(side == 1)(links[F, c].wait_send)
        for j in range(2):
            if c in FORWARD:
                pl.when(side == 0)(links[S1 + j, c].wait_send)
            else:
                links[S1 + j, c].wait_send()
    for kind in (XP, XD, XQ, XG):
        swaps[kind][1].wait_send()
    bias_swap.wait_send()
    for i in range(4):
        swaps[XO + i][0].wait()
        swaps[XO + i][1].wait()
    swap.wait_send()
    for copy in around + across:
        copy.wait_send()


def store_kernel(*refs):
    count = (len(refs) - 1) // 2
    copies = [pltpu.make_async_copy(refs[i], refs[count + i], refs[-1].at[i]) for i in range(count)]
    for copy in copies:
        copy.start()
    for copy in copies:
        copy.wait()


def solution(mesh):
    chips = mesh.shape["seq"] // 2
    books = mesh.shape["dp"]

    def local(queries, key_vectors, value_vectors, cotangent, compress_kernel, memory_reach):
        share = 4 * E // (2 * chips)
        shapes = [((SEG, WIDTH), BF)] * 4 + [((share, E), F32)]
        anywhere = pl.BlockSpec(memory_space=pl.ANY)
        local_memory = pl.BlockSpec(memory_space=pltpu.VMEM)
        vm = pltpu.VMEM
        results = pl.pallas_call(
            functools.partial(kernel, chips, books),
            out_shape=tuple(vm(shape, kind) for shape, kind in shapes),
            in_specs=[anywhere] * 5 + [pl.BlockSpec(memory_space=pltpu.SMEM)],
            out_specs=[local_memory] * 5,
            scratch_shapes=[
                vm((SEG, WIDTH), BF), vm((SEG, WIDTH), BF), vm((4 * E, E), BF), vm((2, SEG, SEG), BF),
                vm((H, 2, SEG, E), BF), vm((H, 2, ROWS, E), BF), vm((HALF, 2, 6 * ROWS, E), BF),
                vm((2, HALF, 2, SEG, E), BF), vm((2, 2, SEG, SPAN), BF), vm((2, 2 * SEG, SEG), F32),
                vm((HALF, 2, SEG, E), BF), vm((HALF, 2, ROWS, E), F32), vm((2, HALF, 2, 2 * ROWS, E), BF),
                vm((2, 2, HALF, SEG, E), F32), vm((2, 2, HALF, 2 * SEG, SEG), BF),
                vm((HALF, 2, 2 * ROWS, E), BF), vm((4, 2, SEG, SPAN), BF),
                vm((2, chips, share, E), F32), vm((chips, share, E), F32), vm((chips, share, E), BF),
                vm((chips, share, E), BF), vm((books, share, E), F32),
                pltpu.SemaphoreType.DMA((3,)),
                pltpu.SemaphoreType.DMA((KINDS, NC)), pltpu.SemaphoreType.DMA((KINDS, NC)),
                pltpu.SemaphoreType.DMA((SWAPS,)), pltpu.SemaphoreType.DMA((SWAPS,)), pltpu.SemaphoreType.DMA((SWAPS,)),
                pltpu.SemaphoreType.DMA((chips,)), pltpu.SemaphoreType.DMA((chips,)),
                pltpu.SemaphoreType.DMA((books,)), pltpu.SemaphoreType.DMA((books,)),
            ],
            compiler_params=pltpu.CompilerParams(collective_id=0, has_side_effects=True),
        )(queries, key_vectors, value_vectors, cotangent, compress_kernel, memory_reach)
        results = [pltpu.with_memory_space_constraint(result, pltpu.VMEM) for result in results]
        stored = pl.pallas_call(
            store_kernel,
            out_shape=tuple(jax.ShapeDtypeStruct(shape, kind) for shape, kind in shapes),
            in_specs=[local_memory] * 5,
            out_specs=[anywhere] * 5,
            scratch_shapes=[pltpu.SemaphoreType.DMA((5,))],
        )(*results)
        return tuple(whole[None] for whole in stored[:4]) + (stored[4],)

    rows = P("dp", "seq", None)
    return jax.shard_map(
        local, mesh=mesh, in_specs=(rows, rows, rows, rows, P(), P("dp", "seq")),
        out_specs=(rows, rows, rows, rows, P("seq", None)), check_vma=False,
    )
```

```python
import functools

import jax
import jax.numpy as jnp
from jax import lax
from jax.experimental import pallas as pl
from jax.experimental.pallas import tpu as pltpu
from jax.sharding import PartitionSpec as P

MESH = pl.DeviceIdType.MESH
H = 16
E = 128
SEG = 128
ROWS = SEG // 4
SLOTS = 4
HALF = H // 2
SIZES = (1,) * HALF
NC = len(SIZES)
FIRST = tuple(sum(SIZES[:c]) for c in range(NC))
FORWARD = ()
BACKWARD = ()
LAG = 1
WIDTH = H * E
SPAN = HALF * E
BF = jnp.bfloat16
F32 = jnp.float32
SCALE = E ** -0.5
LOG2E = 1.4426950408889634
S1, S2, F, U1, U2, KINDS = 0, 2, 4, 5, 6, 7
XP, XD, XQ, XG, XB, XO, SWAPS = 0, 1, 2, 3, 4, 5, 9


def nn(a, b):
    return lax.dot_general(a, b, (((1,), (0,)), ((), ())), preferred_element_type=F32)


def nt(a, b):
    return lax.dot_general(a, b, (((1,), (1,)), ((), ())), preferred_element_type=F32)


def tn(a, b):
    return lax.dot_general(a, b, (((0,), (0,)), ((), ())), preferred_element_type=F32)


def kernel(
    chips, books,
    q_hbm, k_hbm, v_hbm, g_hbm, w_hbm, reach,
    att_out, gq_out, gk_out, gv_out, gw_out,
    k_in, v_in, w_in, perms, perm, packed, memory, segments, sides, bias,
    totals, local, arrived, own, kept, summed, results,
    kg_half, kg_pair, kg_sent, kg_got, kg_books,
    load_sem, send_sem, recv_sem, swap_send, swap_recv, swap_local,
    ring_send, ring_recv, book_send, book_recv,
):
    me = lax.axis_index("seq")
    book = lax.axis_index("dp")
    chip = me // 2
    core = me % 2
    side = chip % 2
    twin = me + 1 - 2 * core

    def chip_at(step):
        return (chip + step + chips) % chips

    def seat(step):
        return chip_at(step) * 2 + core

    def half(which):
        return pl.ds(pl.multiple_of(which * SPAN, SPAN), SPAN)

    loads = [
        pltpu.make_async_copy(source, target, load_sem.at[i])
        for i, (source, target) in enumerate([(k_hbm.at[0], k_in), (v_hbm.at[0], v_in), (w_hbm, w_in)])
    ]
    barrier = pltpu.get_barrier_semaphore()

    def greet(**where):
        pl.semaphore_signal(barrier, inc=1, device_id=where, device_id_type=MESH)

    for step in range(books - 1, 0, -1):
        greet(dp=(book + step) % books)
    for step in sorted(range(1, chips), key=lambda one: -min(one, chips - one)):
        greet(seq=seat(step))
    for step in range(1, 3):
        greet(seq=chip_at(step) * 2 + 1 - core)
        greet(seq=chip_at(-step) * 2 + 1 - core)
    greet(seq=twin)
    for load in loads:
        load.start()

    def heads(chunk, which=0):
        return pl.ds(which * HALF + FIRST[chunk], SIZES[chunk])

    def cols(head, count=1):
        return pl.ds(head * E, count * E)

    def push(source, target, sent, got, device):
        return pltpu.make_async_remote_copy(
            src_ref=source, dst_ref=target, send_sem=sent, recv_sem=got,
            device_id={"seq": device}, device_id_type=MESH,
        )

    def rows(c, first, count):
        return memory.at[heads(c), :, pl.ds(first, count)]

    own_row = pl.multiple_of(ROWS * core, ROWS)
    links = {}
    for c in range(NC):
        for j in range(2):
            links[S1 + j, c] = push(
                packed.at[heads(c, j)], rows(c, 2 * ROWS + own_row, ROWS),
                send_sem.at[S1 + j, c], recv_sem.at[S1 + core, c], chip_at(1) * 2 + j,
            )
            links[S2 + j, c] = push(
                packed.at[heads(c, j)], rows(c, own_row, ROWS),
                send_sem.at[S2 + j, c], recv_sem.at[S2 + core, c], chip_at(2) * 2 + j,
            )
        links[F, c] = push(
            rows(c, 0, 2 * ROWS), rows(c, 2 * ROWS, 2 * ROWS), send_sem.at[F, c], recv_sem.at[F, c], seat(-1),
        )
        links[U1, c] = push(
            totals.at[heads(c), :, pl.ds(2 * ROWS, 2 * ROWS)], arrived.at[0, heads(c)],
            send_sem.at[U1, c], recv_sem.at[U1, c], seat(1 - 2 * side) if c in BACKWARD else seat(-1),
        )
        links[U2, c] = push(
            totals.at[heads(c), :, pl.ds(0, 2 * ROWS)], arrived.at[1, heads(c)],
            send_sem.at[U2, c], recv_sem.at[U2, c], seat(-2),
        )

    def landed(kind, c):
        for k in range(2):
            push(
                packed.at[heads(c)], rows(c, 2 * ROWS if kind == S1 else 0, ROWS),
                send_sem.at[kind + k, c], recv_sem.at[kind + k, c], twin,
            ).wait_recv()

    def swap_pair(kind, mine, other, here, there):
        return (
            pltpu.make_async_copy(mine, here, swap_local.at[kind]),
            push(other, there, swap_send.at[kind], swap_recv.at[kind], twin),
        )

    def half_heads(which):
        return pl.ds(which * HALF, HALF)

    mid_rows = memory.at[:, :, pl.ds(4 * ROWS + own_row, ROWS)]
    swaps = {
        XP: swap_pair(XP, perm.at[half_heads(core)], perm.at[half_heads(1 - core)], segments.at[core], segments.at[core]),
        XD: swap_pair(XD, packed.at[half_heads(core)], packed.at[half_heads(1 - core)], mid_rows, mid_rows),
    }
    for kind, source in ((XQ, q_hbm), (XG, g_hbm)):
        target = sides.at[core, kind - XQ]
        swaps[kind] = swap_pair(kind, source.at[0, :, half(core)], source.at[0, :, half(1 - core)], target, target)
    for i, out in enumerate((att_out, gq_out, gk_out, gv_out)):
        target = out.at[:, half(core)]
        swaps[XO + i] = swap_pair(XO + i, results.at[i, core], results.at[i, 1 - core], target, target)
    open_rows = bias.at[core, pl.ds(0, SEG)]
    bias_swap = push(open_rows, open_rows, swap_send.at[XB], swap_recv.at[XB], twin)

    def hand_out(i):
        for copy in swaps[XO + i]:
            copy.start()

    swaps[XQ][0].start()
    swaps[XG][0].start()

    row = lax.broadcasted_iota(jnp.int32, (SEG, SEG), 0)
    col = lax.broadcasted_iota(jnp.int32, (SEG, SEG), 1)
    row_key = 4 * (row % ROWS) + row // ROWS
    col_key = 4 * (col % ROWS) + col // ROWS
    perms[0] = jnp.where(col == row_key, 1.0, 0.0).astype(BF)
    perms[1] = jnp.where(row == col_key, 1.0, 0.0).astype(BF)
    seen = jnp.minimum(reach[0, 0], me)
    bias[core, 0:SEG] = jnp.where(SLOTS - row // ROWS <= seen, 0.0, -1e30)
    causal = jnp.where(row_key <= col, 0.0, -1e30)
    bias[0, SEG:] = causal
    bias[1, SEG:] = causal

    def spread_lanes(one):
        return jnp.concatenate([one[t * ROWS:(t + 1) * ROWS] for t in range(4)], axis=1)

    def compress(c):
        size = SIZES[c]
        lhs, places = [], []
        for j in range(2):
            first = j * HALF + FIRST[c]
            for i, source in enumerate((k_in, v_in)):
                moved = nn(perms[0], source[:, cols(first, size)]).astype(BF)
                for h in range(size):
                    one = moved[:, h * E:(h + 1) * E]
                    perm[first + h, i] = one
                    lhs.append(spread_lanes(one))
                    places.append((first + h, i))
        out = nn(jnp.concatenate(lhs, axis=0), w_in[...]).astype(BF)
        for n, (h, i) in enumerate(places):
            packed[h, i] = out[n * ROWS:(n + 1) * ROWS]

    def listed(p, h, i):
        return jnp.concatenate([memory[h, i, p * ROWS:p * ROWS + SEG], segments[p, h, i]], axis=0)

    def score(h):
        pieces = []
        for p in range(2):
            query = sides[p, 0, :, cols(h)]
            grad = sides[p, 1, :, cols(h)]
            scores = nt(listed(p, h, 0), query) * (SCALE * LOG2E) + bias[p]
            raised = jnp.exp2(scores - jnp.max(scores, axis=0, keepdims=True))
            weights = raised * (1.0 / jnp.sum(raised, axis=0, keepdims=True))
            low = weights.astype(BF)
            grad_weights = nt(listed(p, h, 1), grad)
            delta = jnp.sum(weights * grad_weights, axis=0, keepdims=True)
            grad_scores = (weights * (grad_weights - delta) * SCALE).astype(BF)
            kept[p, 0, h] = grad_scores
            kept[p, 1, h] = low
            pieces.append((nn(grad_scores[:SEG], query), nn(low[:SEG], grad)))
        for i in range(2):
            left, right = pieces[0][i], pieces[1][i]
            totals[h, i, 0:ROWS] = left[:ROWS].astype(BF)
            totals[h, i, ROWS:] = (left[ROWS:] + right[:SEG - ROWS]).astype(BF)
            local[h, i] = right[SEG - ROWS:]

    def attend(h):
        for p in range(2):
            grad_scores, low = kept[p, 0, h], kept[p, 1, h]
            results[0, p, :, cols(h)] = tn(low, listed(p, h, 1)).astype(BF)
            results[1, p, :, cols(h)] = tn(grad_scores, listed(p, h, 0)).astype(BF)
            own[0, p, h] = nn(grad_scores[SEG:], sides[p, 0, :, cols(h)])
            own[1, p, h] = nn(low[SEG:], sides[p, 1, :, cols(h)])

    def combine(c):
        links[U1, c].start()
        if c in BACKWARD:
            pl.when(side == 0)(links[U2, c].start)
        else:
            links[U2, c].start()

    def carry(c):
        if c in BACKWARD:
            links[U1, c].wait_recv()

            @pl.when(side == 1)
            def _():
                totals[heads(c), :, 0:2 * ROWS] = (
                    totals[heads(c), :, 0:2 * ROWS].astype(F32) + arrived[0, heads(c)].astype(F32)
                ).astype(BF)
                links[U2, c].start()

    def chunk_heads(c):
        return range(FIRST[c], FIRST[c] + SIZES[c])

    def gather(c):
        if c not in BACKWARD:
            links[U1, c].wait_recv()
        links[U2, c].wait_recv()
        lhs, rhs = [], []
        for h in chunk_heads(c):
            near = arrived[0, h].astype(F32)
            if c in BACKWARD:
                near = jnp.where(side == 0, near, 0.0)
            whole = near + arrived[1, h].astype(F32)
            for i in range(2):
                one = jnp.concatenate([whole[i, :ROWS] + local[h, i], whole[i, ROWS:]], axis=0).astype(BF)
                summed[h, i] = one
                rhs.append(one)
                for p in range(2):
                    lhs.append(spread_lanes(segments[p, h, i]))
        return tn(jnp.concatenate(lhs, axis=0), jnp.concatenate(rhs, axis=0))

    def finish(c):
        size = SIZES[c]
        back = nt(jnp.concatenate([summed[h, i] for h in chunk_heads(c) for i in range(2)], axis=0), w_in[...])
        for i in range(2):
            for p in range(2):
                pieces = []
                for n, h in enumerate(chunk_heads(c)):
                    start = (4 * n + 2 * i + p) * ROWS
                    wide = jnp.concatenate(
                        [back[start:start + ROWS, t * E:(t + 1) * E] for t in range(4)], axis=0
                    )
                    pieces.append((own[i, p, h] + wide).astype(BF))
                results[2 + i, p, :, cols(FIRST[c], size)] = nn(
                    perms[1], jnp.concatenate(pieces, axis=1)
                ).astype(BF)

    def pass_on(c):
        if c in FORWARD:
            landed(S2, c)
            pl.when(side == 1)(links[F, c].start)

    def ready(c):
        if c in FORWARD:
            pl.when(side == 1)(lambda: landed(S1, c))
            pl.when(side == 0)(links[F, c].wait_recv)
        else:
            landed(S2, c)
            landed(S1, c)

    def send(c):
        for j in range(2):
            if c in FORWARD:
                pl.when(side == 0)(links[S1 + j, c].start)
            else:
                links[S1 + j, c].start()
        for j in range(2):
            links[S2 + j, c].start()

    for load in loads:
        load.wait()
    for c in range(NC):
        compress(c)
        if c == 0:
            pl.semaphore_wait(barrier, chips + books + 3)
        send(c)
        if c == 2:
            for kind in (XQ, XG):
                swaps[kind][1].start()
            bias_swap.start()
    for copy in swaps[XD] + swaps[XP]:
        copy.start()

    pass_on(0)
    pass_on(1)
    for kind in (XP, XD, XQ, XG):
        swaps[kind][0].wait()
        swaps[kind][1].wait_recv()
    bias_swap.wait_recv()
    for c in range(NC):
        if c + 2 < NC:
            pass_on(c + 2)
        ready(c)
        for h in chunk_heads(c):
            score(h)
        combine(c)
        for h in chunk_heads(c):
            attend(h)
        if c >= LAG:
            carry(c - LAG)
    hand_out(0)
    hand_out(1)
    for c in range(NC - LAG, NC):
        carry(c)
    kernel_terms = gather(0)
    finish(0)
    for c in range(1, NC):
        kernel_terms = kernel_terms + gather(c)
        if c + 2 < NC:
            finish(c)

    share = 4 * E // (2 * chips)
    for i in range(2 * chips):
        kg_half[i % 2, i // 2] = kernel_terms[i * share:(i + 1) * share]
    swap = pltpu.make_async_remote_copy(
        src_ref=kg_half.at[1 - core], dst_ref=kg_pair, send_sem=ring_send.at[0], recv_sem=ring_recv.at[0],
        device_id={"seq": twin}, device_id_type=MESH,
    )
    swap.start()
    finish(NC - 2)
    swap.wait_recv()
    kg_sent[...] = (kg_half[core] + kg_pair[...]).astype(BF)
    around = []
    for step in range(1, chips):
        around.append(pltpu.make_async_remote_copy(
            src_ref=kg_sent.at[(chip + step) % chips], dst_ref=kg_got.at[step],
            send_sem=ring_send.at[step], recv_sem=ring_recv.at[step],
            device_id={"seq": seat(step)}, device_id_type=MESH,
        ))
    for step in sorted(range(1, chips), key=lambda one: -min(one, chips - one)):
        around[step - 1].start()
    finish(NC - 1)
    hand_out(2)
    hand_out(3)
    total = kg_sent[chip].astype(F32)
    for step, copy in enumerate(around):
        copy.wait_recv()
        total = total + kg_got[step + 1].astype(F32)
    kg_books[book] = total
    across = []
    for step in range(1, books):
        across.append(pltpu.make_async_remote_copy(
            src_ref=kg_books.at[book], dst_ref=kg_books.at[book],
            send_sem=book_send.at[step], recv_sem=book_recv.at[step],
            device_id={"dp": (book + step) % books}, device_id_type=MESH,
        ))
    for copy in across[::-1]:
        copy.start()
    for copy in across:
        copy.wait_recv()
    whole = kg_books[0]
    for i in range(1, books):
        whole = whole + kg_books[i]
    gw_out[...] = whole
    for c in range(NC):
        for kind in (S2, S2 + 1, U1, U2):
            links[kind, c].wait_send()
        if c in FORWARD:
            pl.when(side == 1)(links[F, c].wait_send)
        for j in range(2):
            if c in FORWARD:
                pl.when(side == 0)(links[S1 + j, c].wait_send)
            else:
                links[S1 + j, c].wait_send()
    for kind in (XP, XD, XQ, XG):
        swaps[kind][1].wait_send()
    bias_swap.wait_send()
    for i in range(4):
        swaps[XO + i][0].wait()
        swaps[XO + i][1].wait()
    swap.wait_send()
    for copy in around + across:
        copy.wait_send()


def store_kernel(*refs):
    count = (len(refs) - 1) // 2
    copies = [pltpu.make_async_copy(refs[i], refs[count + i], refs[-1].at[i]) for i in range(count)]
    for copy in copies:
        copy.start()
    for copy in copies:
        copy.wait()


def solution(mesh):
    chips = mesh.shape["seq"] // 2
    books = mesh.shape["dp"]

    def local(queries, key_vectors, value_vectors, cotangent, compress_kernel, memory_reach):
        share = 4 * E // (2 * chips)
        shapes = [((SEG, WIDTH), BF)] * 4 + [((share, E), F32)]
        anywhere = pl.BlockSpec(memory_space=pl.ANY)
        local_memory = pl.BlockSpec(memory_space=pltpu.VMEM)
        vm = pltpu.VMEM
        results = pl.pallas_call(
            functools.partial(kernel, chips, books),
            out_shape=tuple(vm(shape, kind) for shape, kind in shapes),
            in_specs=[anywhere] * 5 + [pl.BlockSpec(memory_space=pltpu.SMEM)],
            out_specs=[local_memory] * 5,
            scratch_shapes=[
                vm((SEG, WIDTH), BF), vm((SEG, WIDTH), BF), vm((4 * E, E), BF), vm((2, SEG, SEG), BF),
                vm((H, 2, SEG, E), BF), vm((H, 2, ROWS, E), BF), vm((HALF, 2, 6 * ROWS, E), BF),
                vm((2, HALF, 2, SEG, E), BF), vm((2, 2, SEG, SPAN), BF), vm((2, 2 * SEG, SEG), F32),
                vm((HALF, 2, SEG, E), BF), vm((HALF, 2, ROWS, E), F32), vm((2, HALF, 2, 2 * ROWS, E), BF),
                vm((2, 2, HALF, SEG, E), F32), vm((2, 2, HALF, 2 * SEG, SEG), BF),
                vm((HALF, 2, 2 * ROWS, E), BF), vm((4, 2, SEG, SPAN), BF),
                vm((2, chips, share, E), F32), vm((chips, share, E), F32), vm((chips, share, E), BF),
                vm((chips, share, E), BF), vm((books, share, E), F32),
                pltpu.SemaphoreType.DMA((3,)),
                pltpu.SemaphoreType.DMA((KINDS, NC)), pltpu.SemaphoreType.DMA((KINDS, NC)),
                pltpu.SemaphoreType.DMA((SWAPS,)), pltpu.SemaphoreType.DMA((SWAPS,)), pltpu.SemaphoreType.DMA((SWAPS,)),
                pltpu.SemaphoreType.DMA((chips,)), pltpu.SemaphoreType.DMA((chips,)),
                pltpu.SemaphoreType.DMA((books,)), pltpu.SemaphoreType.DMA((books,)),
            ],
            compiler_params=pltpu.CompilerParams(collective_id=0, has_side_effects=True),
        )(queries, key_vectors, value_vectors, cotangent, compress_kernel, memory_reach)
        results = [pltpu.with_memory_space_constraint(result, pltpu.VMEM) for result in results]
        stored = pl.pallas_call(
            store_kernel,
            out_shape=tuple(jax.ShapeDtypeStruct(shape, kind) for shape, kind in shapes),
            in_specs=[local_memory] * 5,
            out_specs=[anywhere] * 5,
            scratch_shapes=[pltpu.SemaphoreType.DMA((5,))],
        )(*results)
        return tuple(whole[None] for whole in stored[:4]) + (stored[4],)

    rows = P("dp", "seq", None)
    return jax.shard_map(
        local, mesh=mesh, in_specs=(rows, rows, rows, rows, P(), P("dp", "seq")),
        out_specs=(rows, rows, rows, rows, P("seq", None)), check_vma=False,
    )
```

```python
import functools

import jax
import jax.numpy as jnp
from jax import lax
from jax.experimental import pallas as pl
from jax.experimental.pallas import tpu as pltpu
from jax.sharding import PartitionSpec as P

MESH = pl.DeviceIdType.MESH
H = 16
E = 128
SEG = 128
ROWS = SEG // 4
SLOTS = 4
HALF = H // 2
SIZES = (1,) * HALF
NC = len(SIZES)
FIRST = tuple(sum(SIZES[:c]) for c in range(NC))
FORWARD = ()
BACKWARD = ()
LAG = 1
WIDTH = H * E
SPAN = HALF * E
BF = jnp.bfloat16
F32 = jnp.float32
SCALE = E ** -0.5
LOG2E = 1.4426950408889634
S1, S2, F, U1, U2, KINDS = 0, 2, 4, 5, 6, 7
XP, XD, XQ, XG, XB, XO, SWAPS = 0, 1, 2, 3, 4, 5, 9


def nn(a, b):
    return lax.dot_general(a, b, (((1,), (0,)), ((), ())), preferred_element_type=F32)


def nt(a, b):
    return lax.dot_general(a, b, (((1,), (1,)), ((), ())), preferred_element_type=F32)


def tn(a, b):
    return lax.dot_general(a, b, (((0,), (0,)), ((), ())), preferred_element_type=F32)


def kernel(
    chips, books,
    q_hbm, k_hbm, v_hbm, g_hbm, w_hbm, reach,
    att_out, gq_out, gk_out, gv_out, gw_out,
    k_in, v_in, w_in, perms, perm, packed, memory, segments, sides, bias,
    totals, local, arrived, own, kept, summed, results,
    kg_half, kg_pair, kg_sent, kg_got, kg_books,
    load_sem, send_sem, recv_sem, swap_send, swap_recv, swap_local,
    ring_send, ring_recv, book_send, book_recv,
):
    me = lax.axis_index("seq")
    book = lax.axis_index("dp")
    chip = me // 2
    core = me % 2
    side = chip % 2
    twin = me + 1 - 2 * core

    def chip_at(step):
        return (chip + step + chips) % chips

    def seat(step):
        return chip_at(step) * 2 + core

    def half(which):
        return pl.ds(pl.multiple_of(which * SPAN, SPAN), SPAN)

    loads = [
        pltpu.make_async_copy(source, target, load_sem.at[i])
        for i, (source, target) in enumerate([(k_hbm.at[0], k_in), (v_hbm.at[0], v_in), (w_hbm, w_in)])
    ]
    barrier = pltpu.get_barrier_semaphore()

    def greet(**where):
        pl.semaphore_signal(barrier, inc=1, device_id=where, device_id_type=MESH)

    for step in range(books - 1, 0, -1):
        greet(dp=(book + step) % books)
    for step in sorted(range(1, chips), key=lambda one: -min(one, chips - one)):
        greet(seq=seat(step))
    for step in range(1, 3):
        greet(seq=chip_at(step) * 2 + 1 - core)
        greet(seq=chip_at(-step) * 2 + 1 - core)
    greet(seq=twin)
    for load in loads:
        load.start()

    def heads(chunk, which=0):
        return pl.ds(which * HALF + FIRST[chunk], SIZES[chunk])

    def cols(head, count=1):
        return pl.ds(head * E, count * E)

    def push(source, target, sent, got, device):
        return pltpu.make_async_remote_copy(
            src_ref=source, dst_ref=target, send_sem=sent, recv_sem=got,
            device_id={"seq": device}, device_id_type=MESH,
        )

    def rows(c, first, count):
        return memory.at[heads(c), :, pl.ds(first, count)]

    own_row = pl.multiple_of(ROWS * core, ROWS)
    links = {}
    for c in range(NC):
        for j in range(2):
            links[S1 + j, c] = push(
                packed.at[heads(c, j)], rows(c, 2 * ROWS + own_row, ROWS),
                send_sem.at[S1 + j, c], recv_sem.at[S1 + core, c], chip_at(1) * 2 + j,
            )
            links[S2 + j, c] = push(
                packed.at[heads(c, j)], rows(c, own_row, ROWS),
                send_sem.at[S2 + j, c], recv_sem.at[S2 + core, c], chip_at(2) * 2 + j,
            )
        links[F, c] = push(
            rows(c, 0, 2 * ROWS), rows(c, 2 * ROWS, 2 * ROWS), send_sem.at[F, c], recv_sem.at[F, c], seat(-1),
        )
        links[U1, c] = push(
            totals.at[heads(c), :, pl.ds(2 * ROWS, 2 * ROWS)], arrived.at[0, heads(c)],
            send_sem.at[U1, c], recv_sem.at[U1, c], seat(1 - 2 * side) if c in BACKWARD else seat(-1),
        )
        links[U2, c] = push(
            totals.at[heads(c), :, pl.ds(0, 2 * ROWS)], arrived.at[1, heads(c)],
            send_sem.at[U2, c], recv_sem.at[U2, c], seat(-2),
        )

    def landed(kind, c):
        for k in range(2):
            push(
                packed.at[heads(c)], rows(c, 2 * ROWS if kind == S1 else 0, ROWS),
                send_sem.at[kind + k, c], recv_sem.at[kind + k, c], twin,
            ).wait_recv()

    def swap_pair(kind, mine, other, here, there):
        return (
            pltpu.make_async_copy(mine, here, swap_local.at[kind]),
            push(other, there, swap_send.at[kind], swap_recv.at[kind], twin),
        )

    def half_heads(which):
        return pl.ds(which * HALF, HALF)

    mid_rows = memory.at[:, :, pl.ds(4 * ROWS + own_row, ROWS)]
    swaps = {
        XP: swap_pair(XP, perm.at[half_heads(core)], perm.at[half_heads(1 - core)], segments.at[core], segments.at[core]),
        XD: swap_pair(XD, packed.at[half_heads(core)], packed.at[half_heads(1 - core)], mid_rows, mid_rows),
    }
    for kind, source in ((XQ, q_hbm), (XG, g_hbm)):
        target = sides.at[core, kind - XQ]
        swaps[kind] = swap_pair(kind, source.at[0, :, half(core)], source.at[0, :, half(1 - core)], target, target)
    for i, out in enumerate((att_out, gq_out, gk_out, gv_out)):
        target = out.at[:, half(core)]
        swaps[XO + i] = swap_pair(XO + i, results.at[i, core], results.at[i, 1 - core], target, target)
    open_rows = bias.at[core, pl.ds(0, SEG)]
    bias_swap = push(open_rows, open_rows, swap_send.at[XB], swap_recv.at[XB], twin)

    def hand_out(i):
        for copy in swaps[XO + i]:
            copy.start()

    swaps[XQ][0].start()
    swaps[XG][0].start()

    row = lax.broadcasted_iota(jnp.int32, (SEG, SEG), 0)
    col = lax.broadcasted_iota(jnp.int32, (SEG, SEG), 1)
    row_key = 4 * (row % ROWS) + row // ROWS
    col_key = 4 * (col % ROWS) + col // ROWS
    perms[0] = jnp.where(col == row_key, 1.0, 0.0).astype(BF)
    perms[1] = jnp.where(row == col_key, 1.0, 0.0).astype(BF)
    seen = jnp.minimum(reach[0, 0], me)
    bias[core, 0:SEG] = jnp.where(SLOTS - row // ROWS <= seen, 0.0, -1e30)
    causal = jnp.where(row_key <= col, 0.0, -1e30)
    bias[0, SEG:] = causal
    bias[1, SEG:] = causal

    def spread_lanes(one):
        return jnp.concatenate([one[t * ROWS:(t + 1) * ROWS] for t in range(4)], axis=1)

    def compress(c):
        size = SIZES[c]
        lhs, places = [], []
        for j in range(2):
            first = j * HALF + FIRST[c]
            for i, source in enumerate((k_in, v_in)):
                moved = nn(perms[0], source[:, cols(first, size)]).astype(BF)
                for h in range(size):
                    one = moved[:, h * E:(h + 1) * E]
                    perm[first + h, i] = one
                    lhs.append(spread_lanes(one))
                    places.append((first + h, i))
        out = nn(jnp.concatenate(lhs, axis=0), w_in[...]).astype(BF)
        for n, (h, i) in enumerate(places):
            packed[h, i] = out[n * ROWS:(n + 1) * ROWS]

    def listed(p, h, i):
        return jnp.concatenate([memory[h, i, p * ROWS:p * ROWS + SEG], segments[p, h, i]], axis=0)

    def score(h):
        pieces = []
        for p in range(2):
            query = sides[p, 0, :, cols(h)]
            grad = sides[p, 1, :, cols(h)]
            scores = nt(listed(p, h, 0), query) * (SCALE * LOG2E) + bias[p]
            raised = jnp.exp2(scores - jnp.max(scores, axis=0, keepdims=True))
            weights = raised * (1.0 / jnp.sum(raised, axis=0, keepdims=True))
            low = weights.astype(BF)
            grad_weights = nt(listed(p, h, 1), grad)
            delta = jnp.sum(weights * grad_weights, axis=0, keepdims=True)
            grad_scores = (weights * (grad_weights - delta) * SCALE).astype(BF)
            kept[p, 0, h] = grad_scores
            kept[p, 1, h] = low
            pieces.append((nn(grad_scores[:SEG], query), nn(low[:SEG], grad)))
        for i in range(2):
            left, right = pieces[0][i], pieces[1][i]
            totals[h, i, 0:ROWS] = left[:ROWS].astype(BF)
            totals[h, i, ROWS:] = (left[ROWS:] + right[:SEG - ROWS]).astype(BF)
            local[h, i] = right[SEG - ROWS:]

    def attend(h):
        for p in range(2):
            grad_scores, low = kept[p, 0, h], kept[p, 1, h]
            results[0, p, :, cols(h)] = tn(low, listed(p, h, 1)).astype(BF)
            results[1, p, :, cols(h)] = tn(grad_scores, listed(p, h, 0)).astype(BF)
            own[0, p, h] = nn(grad_scores[SEG:], sides[p, 0, :, cols(h)])
            own[1, p, h] = nn(low[SEG:], sides[p, 1, :, cols(h)])

    def combine(c):
        links[U1, c].start()
        if c in BACKWARD:
            pl.when(side == 0)(links[U2, c].start)
        else:
            links[U2, c].start()

    def carry(c):
        if c in BACKWARD:
            links[U1, c].wait_recv()

            @pl.when(side == 1)
            def _():
                totals[heads(c), :, 0:2 * ROWS] = (
                    totals[heads(c), :, 0:2 * ROWS].astype(F32) + arrived[0, heads(c)].astype(F32)
                ).astype(BF)
                links[U2, c].start()

    def chunk_heads(c):
        return range(FIRST[c], FIRST[c] + SIZES[c])

    def gather(c):
        if c not in BACKWARD:
            links[U1, c].wait_recv()
        links[U2, c].wait_recv()
        lhs, rhs = [], []
        for h in chunk_heads(c):
            near = arrived[0, h].astype(F32)
            if c in BACKWARD:
                near = jnp.where(side == 0, near, 0.0)
            whole = near + arrived[1, h].astype(F32)
            for i in range(2):
                one = jnp.concatenate([whole[i, :ROWS] + local[h, i], whole[i, ROWS:]], axis=0).astype(BF)
                summed[h, i] = one
                rhs.append(one)
                for p in range(2):
                    lhs.append(spread_lanes(segments[p, h, i]))
        return tn(jnp.concatenate(lhs, axis=0), jnp.concatenate(rhs, axis=0))

    def finish(c):
        size = SIZES[c]
        back = nt(jnp.concatenate([summed[h, i] for h in chunk_heads(c) for i in range(2)], axis=0), w_in[...])
        for i in range(2):
            for p in range(2):
                pieces = []
                for n, h in enumerate(chunk_heads(c)):
                    start = (4 * n + 2 * i + p) * ROWS
                    wide = jnp.concatenate(
                        [back[start:start + ROWS, t * E:(t + 1) * E] for t in range(4)], axis=0
                    )
                    pieces.append((own[i, p, h] + wide).astype(BF))
                results[2 + i, p, :, cols(FIRST[c], size)] = nn(
                    perms[1], jnp.concatenate(pieces, axis=1)
                ).astype(BF)

    def pass_on(c):
        if c in FORWARD:
            landed(S2, c)
            pl.when(side == 1)(links[F, c].start)

    def ready(c):
        if c in FORWARD:
            pl.when(side == 1)(lambda: landed(S1, c))
            pl.when(side == 0)(links[F, c].wait_recv)
        else:
            landed(S2, c)
            landed(S1, c)

    def send(c):
        for j in range(2):
            if c in FORWARD:
                pl.when(side == 0)(links[S1 + j, c].start)
            else:
                links[S1 + j, c].start()
        for j in range(2):
            links[S2 + j, c].start()

    for load in loads:
        load.wait()
    for c in range(NC):
        compress(c)
        if c == 0:
            pl.semaphore_wait(barrier, chips + books + 3)
        send(c)
        if c == 2:
            for kind in (XQ, XG):
                swaps[kind][1].start()
            bias_swap.start()
    for copy in swaps[XD] + swaps[XP]:
        copy.start()

    pass_on(0)
    pass_on(1)
    for kind in (XP, XD, XQ, XG):
        swaps[kind][0].wait()
        swaps[kind][1].wait_recv()
    bias_swap.wait_recv()
    for c in range(NC):
        if c + 2 < NC:
            pass_on(c + 2)
        ready(c)
        for h in chunk_heads(c):
            score(h)
        combine(c)
        if c >= 1:
            for h in chunk_heads(c - 1):
                attend(h)
        if c >= LAG:
            carry(c - LAG)
    for h in chunk_heads(NC - 1):
        attend(h)
    hand_out(0)
    hand_out(1)
    for c in range(NC - LAG, NC):
        carry(c)
    kernel_terms = gather(0)
    finish(0)
    for c in range(1, NC):
        kernel_terms = kernel_terms + gather(c)
        if c + 2 < NC:
            finish(c)

    share = 4 * E // (2 * chips)
    for i in range(2 * chips):
        kg_half[i % 2, i // 2] = kernel_terms[i * share:(i + 1) * share]
    swap = pltpu.make_async_remote_copy(
        src_ref=kg_half.at[1 - core], dst_ref=kg_pair, send_sem=ring_send.at[0], recv_sem=ring_recv.at[0],
        device_id={"seq": twin}, device_id_type=MESH,
    )
    swap.start()
    finish(NC - 2)
    swap.wait_recv()
    kg_sent[...] = (kg_half[core] + kg_pair[...]).astype(BF)
    around = []
    for step in range(1, chips):
        around.append(pltpu.make_async_remote_copy(
            src_ref=kg_sent.at[(chip + step) % chips], dst_ref=kg_got.at[step],
            send_sem=ring_send.at[step], recv_sem=ring_recv.at[step],
            device_id={"seq": seat(step)}, device_id_type=MESH,
        ))
    for step in sorted(range(1, chips), key=lambda one: -min(one, chips - one)):
        around[step - 1].start()
    finish(NC - 1)
    hand_out(2)
    hand_out(3)
    total = kg_sent[chip].astype(F32)
    for step, copy in enumerate(around):
        copy.wait_recv()
        total = total + kg_got[step + 1].astype(F32)
    kg_books[book] = total
    across = []
    for step in range(1, books):
        across.append(pltpu.make_async_remote_copy(
            src_ref=kg_books.at[book], dst_ref=kg_books.at[book],
            send_sem=book_send.at[step], recv_sem=book_recv.at[step],
            device_id={"dp": (book + step) % books}, device_id_type=MESH,
        ))
    for copy in across[::-1]:
        copy.start()
    for copy in across:
        copy.wait_recv()
    whole = kg_books[0]
    for i in range(1, books):
        whole = whole + kg_books[i]
    gw_out[...] = whole
    for c in range(NC):
        for kind in (S2, S2 + 1, U1, U2):
            links[kind, c].wait_send()
        if c in FORWARD:
            pl.when(side == 1)(links[F, c].wait_send)
        for j in range(2):
            if c in FORWARD:
                pl.when(side == 0)(links[S1 + j, c].wait_send)
            else:
                links[S1 + j, c].wait_send()
    for kind in (XP, XD, XQ, XG):
        swaps[kind][1].wait_send()
    bias_swap.wait_send()
    for i in range(4):
        swaps[XO + i][0].wait()
        swaps[XO + i][1].wait()
    swap.wait_send()
    for copy in around + across:
        copy.wait_send()


def store_kernel(*refs):
    count = (len(refs) - 1) // 2
    copies = [pltpu.make_async_copy(refs[i], refs[count + i], refs[-1].at[i]) for i in range(count)]
    for copy in copies:
        copy.start()
    for copy in copies:
        copy.wait()


def solution(mesh):
    chips = mesh.shape["seq"] // 2
    books = mesh.shape["dp"]

    def local(queries, key_vectors, value_vectors, cotangent, compress_kernel, memory_reach):
        share = 4 * E // (2 * chips)
        shapes = [((SEG, WIDTH), BF)] * 4 + [((share, E), F32)]
        anywhere = pl.BlockSpec(memory_space=pl.ANY)
        local_memory = pl.BlockSpec(memory_space=pltpu.VMEM)
        vm = pltpu.VMEM
        results = pl.pallas_call(
            functools.partial(kernel, chips, books),
            out_shape=tuple(vm(shape, kind) for shape, kind in shapes),
            in_specs=[anywhere] * 5 + [pl.BlockSpec(memory_space=pltpu.SMEM)],
            out_specs=[local_memory] * 5,
            scratch_shapes=[
                vm((SEG, WIDTH), BF), vm((SEG, WIDTH), BF), vm((4 * E, E), BF), vm((2, SEG, SEG), BF),
                vm((H, 2, SEG, E), BF), vm((H, 2, ROWS, E), BF), vm((HALF, 2, 6 * ROWS, E), BF),
                vm((2, HALF, 2, SEG, E), BF), vm((2, 2, SEG, SPAN), BF), vm((2, 2 * SEG, SEG), F32),
                vm((HALF, 2, SEG, E), BF), vm((HALF, 2, ROWS, E), F32), vm((2, HALF, 2, 2 * ROWS, E), BF),
                vm((2, 2, HALF, SEG, E), F32), vm((2, 2, HALF, 2 * SEG, SEG), BF),
                vm((HALF, 2, 2 * ROWS, E), BF), vm((4, 2, SEG, SPAN), BF),
                vm((2, chips, share, E), F32), vm((chips, share, E), F32), vm((chips, share, E), BF),
                vm((chips, share, E), BF), vm((books, share, E), F32),
                pltpu.SemaphoreType.DMA((3,)),
                pltpu.SemaphoreType.DMA((KINDS, NC)), pltpu.SemaphoreType.DMA((KINDS, NC)),
                pltpu.SemaphoreType.DMA((SWAPS,)), pltpu.SemaphoreType.DMA((SWAPS,)), pltpu.SemaphoreType.DMA((SWAPS,)),
                pltpu.SemaphoreType.DMA((chips,)), pltpu.SemaphoreType.DMA((chips,)),
                pltpu.SemaphoreType.DMA((books,)), pltpu.SemaphoreType.DMA((books,)),
            ],
            compiler_params=pltpu.CompilerParams(collective_id=0, has_side_effects=True),
        )(queries, key_vectors, value_vectors, cotangent, compress_kernel, memory_reach)
        results = [pltpu.with_memory_space_constraint(result, pltpu.VMEM) for result in results]
        stored = pl.pallas_call(
            store_kernel,
            out_shape=tuple(jax.ShapeDtypeStruct(shape, kind) for shape, kind in shapes),
            in_specs=[local_memory] * 5,
            out_specs=[anywhere] * 5,
            scratch_shapes=[pltpu.SemaphoreType.DMA((5,))],
        )(*results)
        return tuple(whole[None] for whole in stored[:4]) + (stored[4],)

    rows = P("dp", "seq", None)
    return jax.shard_map(
        local, mesh=mesh, in_specs=(rows, rows, rows, rows, P(), P("dp", "seq")),
        out_specs=(rows, rows, rows, rows, P("seq", None)), check_vma=False,
    )
```
